256 devices in a mesh: along: 32 (over z, x), cross: 2 (over core), batch: 4 (over y).
Axes of the slice: x: 4, y: 4, z: 8, core: 2. Of those that a mesh axis runs over, the one named last changes fastest.
Arguments:
- pressure_start: float32 [4, 16, 2048, 256], P('batch', None, 'along', 'cross'), may hold values from -6 to 6
- along_start: float32 [4, 16, 2048, 256], P('batch', None, 'along', 'cross'), may hold values from -6 to 6
- cross_start: float32 [4, 16, 2048, 256], P('batch', None, 'along', 'cross'), may hold values from -6 to 6
- depth_layers: int32 [2048, 256], P('along', 'cross'), may hold values from 1 to 16
- stiffness: float32 [2048, 256], P('along', 'cross'), may hold values from 0.1 to 0.45
- patch_lists: int32 [4, 4096], P('batch'), may hold values from 0 to 8191, all different within a row
- owner_map: int32 [64, 128], P(('along', 'cross')), may hold values from 0 to 63, as said below
Outputs:
- adjoint_pressure: float32 [4, 16, 2048, 256], P('batch', None, 'along', 'cross')
- panel_store: float32 [64, 192, 4, 512], P(('along', 'cross'), None, 'batch')
The draws below stay inside these ranges and needn't reach their ends.
Inputs may be any that keep to these rules, and one draw needn't show every extreme that they name: `owner_map`: each entry is an owner, numbered as the grid blocks. Of the 128 patches of one block at most 3 have one owner, and in every draw some owner holds exactly 3 patches of every block. `patch_lists`: each row names 4096 different patch ids; every patch is named by some row.
All inputs are finite; a program needn't handle non-finite values.
Results may differ from the reference program's by a relative error of at most 0.0003.
Values sent between devices are 32-bit elements; how exact they have to be, the bound alone decides.
A program may use at most 64 MiB of HBM per device.

```python
import math
import jax
import jax.numpy as jnp
from jax import lax

A_DEV = 64
C_DEV = 128
NZ = 16
STEPS = 8
S = 4
NA = 2048
NC = 256
PC = 64
NP_DEV = 128
OWNERS = 64
NPATCH = 8192
K = 4096
ROUNDS = 2
CAP = 3
SLOTS = 192
TP = 512
N_CROSS = 2


def draw_owner_map(key, part):
    global_key, rows_key = jax.random.split(jax.random.fold_in(key, 11))
    order = jax.random.permutation(global_key, OWNERS)
    hot_owners = order[:4]
    cold_owners = order[4:]

    def one_block(block_key):
        keys = jax.random.split(block_key, ROUNDS + 3)
        rounds = [jax.random.permutation(keys[r], OWNERS) for r in range(ROUNDS - 1)]
        mixed = jax.random.permutation(keys[ROUNDS - 1], cold_owners)
        flips = jax.random.randint(keys[ROUNDS], (3,), 0, 2)
        picks = jnp.where(flips == 1, hot_owners[1:], mixed[OWNERS - 8:OWNERS - 5])
        final_round = jnp.concatenate([hot_owners[0:1], hot_owners[0:1], hot_owners[1:2], picks[0:1], hot_owners[2:3], picks[1:2], hot_owners[3:4], picks[2:3], mixed[:OWNERS - 8]])
        every = jnp.concatenate(rounds + [final_round])
        shuffle = jax.random.permutation(keys[ROUNDS + 1], NP_DEV)
        return every[shuffle]
    return jax.vmap(one_block)(jax.random.split(rows_key, OWNERS)).astype(jnp.int32)


def set_ends(entries, stream_key, least, top_value):
    dims = entries.shape
    index_at = [jax.random.randint(jax.random.fold_in(stream_key, axis), (), 0, dims[axis]) for axis in range(len(dims))]
    entries = entries.at[tuple(index_at)].set(least)
    longest = dims.index(max(dims))
    index_at[longest] = (index_at[longest] + 1) % dims[longest]
    return entries.at[tuple(index_at)].set(top_value)


def block_scale(rng, shape, cuts, smallest, largest):
    def one(axis_at, shards_of):
        heights = jax.random.uniform(jax.random.fold_in(jax.random.fold_in(rng, 6), axis_at), (shards_of,), jnp.float32, smallest / len(cuts), largest / len(cuts))
        return jnp.repeat(jnp.exp(heights), shape[axis_at] // shards_of).reshape((-1,) + (1,) * (len(shape) - axis_at - 1))

    gain = one(*cuts[0])
    for cut in cuts[1:]:
        gain = gain * one(*cut)
    return gain


def different_ones(own_key, rows, number_of, top, lift):
    ranking = jax.random.permutation(jax.random.fold_in(own_key, 1), number_of)
    pull = ranking
    for power in range(3):
        pull = pull * pull // number_of
    pull = pull * lift // number_of
    lots = jax.random.randint(jax.random.fold_in(own_key, 2), (rows, number_of), 0, 4096) + pull
    holders = jax.random.permutation(jax.random.fold_in(own_key, 3), rows)[jnp.arange(number_of) % rows]
    lots = jnp.where(jnp.arange(rows)[:, None] == holders[None, :], 1 << 14, lots)
    merit = lots * number_of + jnp.arange(number_of)
    return lax.top_k(merit.astype(jnp.int32), top)[1].astype(jnp.int32)


def gaussian(rng, extent, spread, limit, cuts=(), kind=jnp.bfloat16):
    values = jax.random.normal(rng, extent, jnp.float32) * spread
    if len(cuts) > 0:
        values = block_scale(rng, extent, cuts, -0.22, 0.18) * values
    return jnp.clip(values, min=-limit, max=limit).astype(kind)


def setup_inputs(seed: int = 0) -> dict:
    seeds = jax.random.split(jax.random.key(seed), 8)
    pressure_start = gaussian(seeds[0], (S, NZ, NA, NC), 1.0, 6.0, ((0, 4), (2, 32), (3, 2)), jnp.float32)
    along_start = gaussian(seeds[1], (S, NZ, NA, NC), 1.0, 6.0, ((0, 4), (2, 32), (3, 2)), jnp.float32)
    cross_start = gaussian(seeds[2], (S, NZ, NA, NC), 1.0, 6.0, ((0, 4), (2, 32), (3, 2)), jnp.float32)
    depth_layers = set_ends(jax.random.randint(seeds[3], (NA, NC), 1, NZ + 1), jax.random.fold_in(seeds[3], 1), 1, NZ).astype(jnp.int32)
    stiffness = jnp.clip(jnp.exp(math.log(0.45) - 1.50407736 * jax.random.uniform(seeds[4], (NA, NC), jnp.float32) ** block_scale(seeds[4], (NA, NC), ((0, 32), (1, 2)), -0.2, 0.2)), 0.1, 0.45)
    patch_lists = different_ones(seeds[5], S, NPATCH, K, 0)
    owner_map = draw_owner_map(jax.random.fold_in(seeds[7], 71), 0)
    return dict(pressure_start=pressure_start, along_start=along_start, cross_start=cross_start, depth_layers=depth_layers, stiffness=stiffness, patch_lists=patch_lists, owner_map=owner_map)


def advance(fields, wet_mask, wet_upper, wet_lower, stiffness, onehot):
    pressure, flow_along, flow_cross = fields
    zero_row = jnp.zeros((NZ, 1, NC), jnp.float32)
    zero_col = jnp.zeros((NZ, NA, 1), jnp.float32)
    zero_layer = jnp.zeros((1, NA, NC), jnp.float32)
    traces = []
    for step_index in range(STEPS):
        ahead_row = jnp.concatenate([pressure[:, 1:, :], zero_row], 1)
        flow_along = wet_mask * (flow_along - (ahead_row - pressure))
        ahead_col = jnp.concatenate([pressure[:, :, 1:], zero_col], 2)
        flow_cross = wet_mask * (flow_cross - (ahead_col - pressure))
        behind = jnp.concatenate([zero_row, flow_along[:, :-1, :]], 1)
        before = jnp.concatenate([zero_col, flow_cross[:, :, :-1]], 2)
        upper_layer = jnp.concatenate([zero_layer, pressure[:-1]], 0)
        lower_layer = jnp.concatenate([pressure[1:], zero_layer], 0)
        vertical = wet_upper * (upper_layer - pressure) + wet_lower * (lower_layer - pressure)
        pressure = wet_mask * (pressure - stiffness * ((flow_along - behind) + (flow_cross - before)) + 0.5 * stiffness * vertical)
        traces.append(jnp.sum(pressure * onehot, axis=0))
    return pressure, jnp.stack(traces)


def reference(pressure_start, along_start, cross_start, depth_layers, stiffness, patch_lists, owner_map):
    layer_index = lax.broadcasted_iota(jnp.int32, (NZ, NA, NC), 0)
    wet_mask = (layer_index < depth_layers[None]).astype(jnp.float32)
    onehot = (layer_index == depth_layers[None] - 1).astype(jnp.float32)
    zero_layer = jnp.zeros((1, NA, NC), jnp.float32)
    wet_upper = jnp.concatenate([zero_layer, wet_mask[:-1]], 0)
    wet_lower = jnp.concatenate([wet_mask[1:], zero_layer], 0)

    def run_sensor(fields):
        return advance(fields, wet_mask, wet_upper, wet_lower, stiffness, onehot)

    adjoint_pressure, traces = lax.map(run_sensor, (pressure_start, along_start, cross_start))
    member = jnp.zeros((S, NPATCH), jnp.float32).at[jnp.arange(S, dtype=jnp.int32)[:, None], patch_lists].set(1.0)
    positions = jnp.arange(NP_DEV, dtype=jnp.int32)
    earlier = positions[None, :] < positions[:, None]

    def place_source(source, panel_store):
        source = source.astype(jnp.int32)
        along_block = source // N_CROSS
        cross_block = source % N_CROSS
        zero_index = jnp.zeros((), jnp.int32)
        trace_block = lax.dynamic_slice(traces, (zero_index, zero_index, along_block * A_DEV, cross_block * C_DEV), (S, STEPS, A_DEV, C_DEV))
        member_block = lax.dynamic_slice(member, (zero_index, source * NP_DEV), (S, NP_DEV))
        panels = trace_block.reshape(S, STEPS, NP_DEV, PC) * member_block[:, None, :, None]
        panels = jnp.transpose(panels, (2, 0, 1, 3)).reshape(NP_DEV, S, TP)
        owners = lax.dynamic_index_in_dim(owner_map, source, 0, keepdims=False)
        slot_rank = jnp.sum(((owners[:, None] == owners[None, :]) & earlier).astype(jnp.int32), axis=1)
        return panel_store.at[owners, source * CAP + slot_rank].set(panels)

    panel_store = lax.fori_loop(0, OWNERS, place_source, jnp.zeros((OWNERS, SLOTS, S, TP), jnp.float32))
    return adjoint_pressure, panel_store
```

```python
import functools

import jax
import jax.numpy as jnp
from jax import lax
from jax.experimental import pallas as pl
from jax.experimental.pallas import tpu as pltpu
from jax.sharding import PartitionSpec as P

STEPS = 8
HALO = 8
PAD = 8
MESH = pl.DeviceIdType.MESH


def kernel(
    n_along,
    layers,
    rows,
    cols,
    cap,
    p_hbm,
    fa_hbm,
    fc_hbm,
    d_hbm,
    k_hbm,
    lists_hbm,
    owners_hbm,
    out_p,
    out_s,
    ep,
    ea,
    ec,
    dx,
    kx,
    lists,
    owners,
    place,
    trace,
    trace_out,
    outgoing,
    local_sem,
    halo_send,
    halo_recv,
    trace_send,
    trace_recv,
    panel_send,
    panel_recv,
    final_sem,
):
    i = lax.axis_index("along")
    j = lax.axis_index("cross")
    other = 1 - j
    block = i * 2 + j
    n_owners = 2 * n_along
    half = rows // 2
    ext = half + HALO
    slots = n_owners * cap

    list_copy = pltpu.make_async_copy(lists_hbm, lists, local_sem.at[5])
    owner_copy = pltpu.make_async_copy(owners_hbm, owners, local_sem.at[6])
    list_copy.start()
    owner_copy.start()
    fields = ((p_hbm, ep), (fa_hbm, ea), (fc_hbm, ec), (d_hbm, dx), (k_hbm, kx))

    def take(src, start, count):
        if len(src.shape) == 4:
            return src.at[0, :, pl.ds(start, count), :]
        return src.at[pl.ds(start, count), :]

    def put(dst, side, start, count):
        if len(dst.shape) == 4:
            return dst.at[side, :, pl.ds(start, count), :]
        return dst.at[side, pl.ds(start, count), :]

    def first_row(core):
        return pl.multiple_of((half - HALO) * core, 8)

    def first_slot(core):
        return pl.multiple_of(PAD + HALO - HALO * core, 8)

    own_copies = []
    for index, (src, dst) in enumerate(fields):
        copy = pltpu.make_async_copy(
            take(src, first_row(j), ext), put(dst, j, first_slot(j), ext), local_sem.at[index]
        )
        copy.start()
        own_copies.append(copy)

    barrier = pltpu.get_barrier_semaphore()

    def greet(k, carry):
        o = lax.rem(block + k, n_owners)
        pl.semaphore_signal(
            barrier, inc=1, device_id={"along": o // 2, "cross": lax.rem(o, 2)}, device_id_type=MESH
        )
        return carry

    lax.fori_loop(1, n_owners, greet, 0)

    for index, (src, dst) in enumerate(fields):
        if len(dst.shape) == 4:
            tail = PAD + ext + HALO
            dst[:, :, 0:PAD, :] = jnp.zeros((2, layers, PAD, cols), jnp.float32)
            dst[:, :, tail : tail + PAD, :] = jnp.zeros((2, layers, PAD, cols), jnp.float32)

    list_copy.wait()
    owner_copy.wait()
    patches = 2 * rows
    lane_r = lax.broadcasted_iota(jnp.int32, (patches, patches), 0)
    lane_c = lax.broadcasted_iota(jnp.int32, (patches, patches), 1)
    id_r = 2 * lax.rem(lane_r, rows) + lane_r // rows
    id_c = 2 * lax.rem(lane_c, rows) + lane_c // rows
    wanted = id_r + block * patches
    seen = jnp.zeros((patches, lists.shape[1]), jnp.float32)
    for row in range(lists.shape[0]):
        seen = jnp.where(lists[row : row + 1, :] == wanted, 1.0, seen)
    ones = jnp.ones((8, lists.shape[1]), jnp.bfloat16)
    member = lax.dot_general(
        ones, seen.astype(jnp.bfloat16), (((1,), (1,)), ((), ())), preferred_element_type=jnp.float32
    )
    permute = jnp.where(lane_r == id_c, 1.0, 0.0).astype(jnp.bfloat16)
    owner_rows = jnp.broadcast_to(owners[...].astype(jnp.float32), (8, patches)).astype(jnp.bfloat16)
    owner_of = jnp.dot(owner_rows, permute, preferred_element_type=jnp.float32)
    slot = lax.broadcasted_iota(jnp.int32, (slots, patches), 0)
    slot_owner = slot // cap
    slot_rank = (slot - slot_owner * cap).astype(jnp.float32)
    mine = owner_of[0:1, :] == slot_owner.astype(jnp.float32)
    before = jnp.where(id_r < id_c, 1.0, 0.0).astype(jnp.bfloat16)
    rank = jnp.dot(
        jnp.where(mine, 1.0, 0.0).astype(jnp.bfloat16), before, preferred_element_type=jnp.float32
    )
    held = jnp.where(mine & (rank == slot_rank), jnp.where(member[0:1, :] > 0.5, 1.0, 0.0), 0.0)
    place[...] = held.astype(jnp.bfloat16)

    pl.semaphore_wait(barrier, n_owners - 1)

    after_chip = lax.rem(i + 1, n_along)
    before_chip = lax.rem(i + n_along - 1, n_along)
    sends = []
    for index, (src, dst) in enumerate(fields):
        sends.append(
            pltpu.make_async_remote_copy(
                src_ref=take(src, rows - HALO, HALO),
                dst_ref=put(dst, j, PAD, HALO),
                send_sem=halo_send.at[index, 0],
                recv_sem=halo_recv.at[index, 1 + j],
                device_id={"along": after_chip, "cross": 0},
                device_id_type=MESH,
            )
        )
        sends.append(
            pltpu.make_async_remote_copy(
                src_ref=take(src, 0, HALO),
                dst_ref=put(dst, j, PAD + ext, HALO),
                send_sem=halo_send.at[index, 1],
                recv_sem=halo_recv.at[index, 1 + j],
                device_id={"along": before_chip, "cross": 1},
                device_id_type=MESH,
            )
        )
        sends.append(
            pltpu.make_async_remote_copy(
                src_ref=take(src, first_row(other), ext),
                dst_ref=put(dst, j, first_slot(other), ext),
                send_sem=halo_send.at[index, 2],
                recv_sem=halo_recv.at[index, 0],
                device_id={"cross": other},
                device_id_type=MESH,
            )
        )
    for copy in sends:
        copy.start()
    for copy in own_copies:
        copy.wait()
    for index, (src, dst) in enumerate(fields):
        for source in range(3):
            count = ext if source == 0 else HALO
            pltpu.make_async_copy(
                take(src, 0, count), put(dst, 0, PAD, count), halo_recv.at[index, source]
            ).wait()

    @pl.when((i == 0) & (j == 0))
    def _():
        ep[:, :, PAD : PAD + HALO, :] = jnp.zeros((2, layers, HALO, cols), jnp.float32)
        dx[:, PAD : PAD + HALO, :] = jnp.zeros((2, HALO, cols), jnp.int32)

    @pl.when((i == n_along - 1) & (j == 1))
    def _():
        ep[:, :, PAD + ext : PAD + ext + HALO, :] = jnp.zeros((2, layers, HALO, cols), jnp.float32)
        dx[:, PAD + ext : PAD + ext + HALO, :] = jnp.zeros((2, HALO, cols), jnp.int32)

    lane = lax.broadcasted_iota(jnp.int32, (8, cols), 1)
    first_lane = lane == 0
    last_lane = lane == cols - 1
    low_lanes = lax.broadcasted_iota(jnp.int32, (rows, cols), 1) < cols // 2
    zero = jnp.zeros((8, cols), jnp.float32)
    tiles = (half + 2 * HALO) // 8
    own_tiles = range(HALO // 8, HALO // 8 + half // 8)
    own_start = pl.multiple_of(half * j, 8)

    def trace_copy(t):
        return pltpu.make_async_remote_copy(
            src_ref=trace_out.at[t],
            dst_ref=trace.at[t, pl.ds(own_start, half), :],
            send_sem=trace_send.at[t],
            recv_sem=trace_recv.at[t],
            device_id={"cross": other},
            device_id_type=MESH,
        )

    def step(t):
        for tile in range(tiles):
            r = PAD + 8 * tile
            depth = [dx[h, r : r + 8, :] for h in range(2)]
            stiff = [kx[h, r : r + 8, :] for h in range(2)]
            half_stiff = [0.5 * stiff[h] for h in range(2)]
            pressure = [ep[h, 0, r : r + 8, :] for h in range(2)]
            wet = [depth[h] > 0 for h in range(2)]
            down = [zero, zero]
            seafloor = [zero, zero]
            for z in range(layers):
                turned = [pltpu.roll(pressure[h], cols - 1, 1) for h in range(2)]
                right = [
                    jnp.where(last_lane, turned[1], turned[0]),
                    jnp.where(last_lane, 0.0, turned[1]),
                ]
                along = []
                cross = []
                for h in range(2):
                    ahead = ep[h, z, r + 1 : r + 9, :]
                    value = jnp.where(wet[h], ea[h, z, r : r + 8, :] - (ahead - pressure[h]), 0.0)
                    ea[h, z, r : r + 8, :] = value
                    along.append(value)
                    value = jnp.where(
                        wet[h], ec[h, z, r : r + 8, :] - (right[h] - pressure[h]), 0.0
                    )
                    ec[h, z, r : r + 8, :] = value
                    cross.append(value)
                turned = [pltpu.roll(cross[h], 1, 1) for h in range(2)]
                left = [
                    jnp.where(first_lane, 0.0, turned[0]),
                    jnp.where(first_lane, turned[0], turned[1]),
                ]
                for h in range(2):
                    behind = ea[h, z, r - 1 : r + 7, :]
                    spread = (along[h] - behind) + (cross[h] - left[h])
                    if z + 1 < layers:
                        lower = ep[h, z + 1, r : r + 8, :]
                        wet_lower = depth[h] > z + 1
                        up = jnp.where(wet_lower, lower - pressure[h], 0.0)
                        vertical = up - down[h]
                    else:
                        vertical = -down[h]
                    value = pressure[h] - stiff[h] * spread + half_stiff[h] * vertical
                    value = jnp.where(wet[h], value, 0.0)
                    ep[h, z, r : r + 8, :] = value
                    seafloor[h] = jnp.where(wet[h], value, seafloor[h])
                    if z + 1 < layers:
                        pressure[h] = lower
                        wet[h] = wet_lower
                        down[h] = up
            if tile in own_tiles:
                at = 8 * (tile - HALO // 8)
                trace[t, pl.ds(pl.multiple_of(own_start + at, 8), 8), :] = jnp.where(
                    j == 0, seafloor[0], seafloor[1]
                )
                trace_out[t, at : at + 8, :] = jnp.where(j == 0, seafloor[1], seafloor[0])
        trace_copy(t).start()

    def panel_copy(g, k):
        o = lax.rem(block + k, n_owners)
        return pltpu.make_async_remote_copy(
            src_ref=outgoing.at[g, pl.ds(o * cap, cap)],
            dst_ref=out_s.at[pl.ds(block * cap, cap), g],
            send_sem=panel_send.at[g],
            recv_sem=panel_recv.at[g],
            device_id={"along": o // 2, "cross": lax.rem(o, 2)},
            device_id_type=MESH,
        )

    def own_panel_copy(g):
        return pltpu.make_async_copy(
            outgoing.at[g, pl.ds(block * cap, cap)],
            out_s.at[pl.ds(block * cap, cap), g],
            final_sem.at[2 + g],
        )

    def send_group(g):
        pair = []
        for s in range(2):
            trace_copy(2 * g + s).wait_recv()
        first, second = trace[2 * g], trace[2 * g + 1]
        left = jnp.where(low_lanes, first, pltpu.roll(second, cols // 2, 1))
        right = jnp.where(low_lanes, pltpu.roll(first, cols // 2, 1), second)
        rest = jnp.concatenate([left, right], 0)
        total = None
        for part in range(3):
            piece = rest.astype(jnp.bfloat16)
            term = jnp.dot(place[...], piece, preferred_element_type=jnp.float32)
            total = term if total is None else total + term
            rest = rest - piece.astype(jnp.float32)
        outgoing[g, :, 0, :] = total
        own_panel_copy(g).start()

        def send(k, carry):
            panel_copy(g, k).start()
            return carry

        lax.fori_loop(1, n_owners, send, 0)

    own_pressure = pltpu.make_async_copy(
        ep.at[j, :, pl.ds(PAD + HALO, half), :],
        out_p.at[0, :, pl.ds(own_start, half), :],
        final_sem.at[0],
    )
    other_pressure = pltpu.make_async_remote_copy(
        src_ref=ep.at[other, :, pl.ds(PAD + HALO, half), :],
        dst_ref=out_p.at[0, :, pl.ds(own_start, half), :],
        send_sem=final_sem.at[1],
        recv_sem=final_sem.at[6],
        device_id={"cross": other},
        device_id_type=MESH,
    )

    def advance(t, carry):
        @pl.when(t < STEPS)
        def _():
            step(t)

        @pl.when(t == STEPS - 1)
        def _():
            own_pressure.start()
            other_pressure.start()

        @pl.when((t >= 2) & (lax.rem(t, 2) == 0))
        def _():
            send_group(t // 2 - 1)

        return carry

    lax.fori_loop(0, STEPS + 1, advance, 0)

    for copy in sends:
        copy.wait_send()
    for t in range(STEPS):
        trace_copy(t).wait_send()
    own_pressure.wait()
    other_pressure.wait()
    moved = (n_owners - 1) * cap
    for g in range(STEPS // 2):
        own_panel_copy(g).wait()
        pltpu.make_async_copy(
            outgoing.at[g, pl.ds(0, moved)], out_s.at[pl.ds(0, moved), g], panel_send.at[g]
        ).wait()
        pltpu.make_async_copy(
            outgoing.at[g, pl.ds(0, moved)], out_s.at[pl.ds(0, moved), g], panel_recv.at[g]
        ).wait()


def shards(
    pressure_start, along_start, cross_start, depth_layers, stiffness, patch_lists, owner_map
):
    _, layers, rows, cols = pressure_start.shape
    n_along = lax.axis_size("along")
    n_owners = n_along * lax.axis_size("cross")
    cap = 2 * rows // n_owners + 1
    slots = n_owners * cap
    ext_rows = rows // 2 + 2 * HALO + 2 * PAD
    lists = patch_lists.reshape(-1, cols)
    any_space = pl.BlockSpec(memory_space=pl.ANY)
    pressure, panels = pl.pallas_call(
        functools.partial(kernel, n_along, layers, rows, cols, cap),
        out_shape=(
            jax.ShapeDtypeStruct(pressure_start.shape, jnp.float32),
            jax.ShapeDtypeStruct((slots, STEPS // 2, 1, cols), jnp.float32),
        ),
        in_specs=[any_space] * 7,
        out_specs=(any_space, any_space),
        scratch_shapes=[
            pltpu.VMEM((2, layers, ext_rows, cols), jnp.float32),
            pltpu.VMEM((2, layers, ext_rows, cols), jnp.float32),
            pltpu.VMEM((2, layers, ext_rows, cols), jnp.float32),
            pltpu.VMEM((2, ext_rows, cols), jnp.int32),
            pltpu.VMEM((2, ext_rows, cols), jnp.float32),
            pltpu.VMEM(lists.shape, jnp.int32),
            pltpu.VMEM(owner_map.shape, jnp.int32),
            pltpu.VMEM((slots, 2 * rows), jnp.bfloat16),
            pltpu.VMEM((STEPS, rows, cols), jnp.float32),
            pltpu.VMEM((STEPS, rows // 2, cols), jnp.float32),
            pltpu.VMEM((STEPS // 2, slots, 1, cols), jnp.float32),
            pltpu.SemaphoreType.DMA((7,)),
            pltpu.SemaphoreType.DMA((5, 3)),
            pltpu.SemaphoreType.DMA((5, 3)),
            pltpu.SemaphoreType.DMA((STEPS,)),
            pltpu.SemaphoreType.DMA((STEPS,)),
            pltpu.SemaphoreType.DMA((STEPS // 2,)),
            pltpu.SemaphoreType.DMA((STEPS // 2,)),
            pltpu.SemaphoreType.DMA((7,)),
        ],
        compiler_params=pltpu.CompilerParams(collective_id=0, has_side_effects=True),
    )(
        pressure_start,
        along_start,
        cross_start,
        depth_layers,
        stiffness,
        lists,
        owner_map,
    )
    return (pressure, panels.reshape(1, slots, 1, STEPS // 2 * cols))


def solution(mesh):
    in_specs = (
        P("batch", None, "along", "cross"),
        P("batch", None, "along", "cross"),
        P("batch", None, "along", "cross"),
        P("along", "cross"),
        P("along", "cross"),
        P("batch", None),
        P(("along", "cross"), None),
    )
    out_specs = (P("batch", None, "along", "cross"), P(("along", "cross"), None, "batch", None))
    return jax.shard_map(shards, mesh=mesh, in_specs=in_specs, out_specs=out_specs, check_vma=False)
```

```python
import functools

import jax
import jax.numpy as jnp
from jax import lax
from jax.experimental import pallas as pl
from jax.experimental.pallas import tpu as pltpu
from jax.sharding import PartitionSpec as P

STEPS = 8
HALO = 8
PAD = 8
MESH = pl.DeviceIdType.MESH


def kernel(
    n_along,
    layers,
    rows,
    cols,
    cap,
    p_hbm,
    fa_hbm,
    fc_hbm,
    d_hbm,
    k_hbm,
    lists_hbm,
    owners_hbm,
    out_p,
    out_s,
    ep,
    ea,
    ec,
    dx,
    kx,
    lists,
    owners,
    place,
    trace,
    trace_out,
    outgoing,
    local_sem,
    halo_send,
    halo_recv,
    trace_send,
    trace_recv,
    panel_send,
    panel_recv,
    final_sem,
):
    i = lax.axis_index("along")
    j = lax.axis_index("cross")
    other = 1 - j
    block = i * 2 + j
    n_owners = 2 * n_along
    half = rows // 2
    ext = half + HALO
    slots = n_owners * cap

    list_copy = pltpu.make_async_copy(lists_hbm, lists, local_sem.at[5])
    owner_copy = pltpu.make_async_copy(owners_hbm, owners, local_sem.at[6])
    list_copy.start()
    owner_copy.start()
    fields = ((p_hbm, ep), (fa_hbm, ea), (fc_hbm, ec), (d_hbm, dx), (k_hbm, kx))

    def take(src, start, count):
        if len(src.shape) == 4:
            return src.at[0, :, pl.ds(start, count), :]
        return src.at[pl.ds(start, count), :]

    def put(dst, side, start, count):
        if len(dst.shape) == 4:
            return dst.at[side, :, pl.ds(start, count), :]
        return dst.at[side, pl.ds(start, count), :]

    def first_row(core):
        return pl.multiple_of((half - HALO) * core, 8)

    def first_slot(core):
        return pl.multiple_of(PAD + HALO - HALO * core, 8)

    own_copies = []
    for index, (src, dst) in enumerate(fields):
        copy = pltpu.make_async_copy(
            take(src, first_row(j), ext), put(dst, j, first_slot(j), ext), local_sem.at[index]
        )
        copy.start()
        own_copies.append(copy)

    barrier = pltpu.get_barrier_semaphore()

    def greet(k, carry):
        o = lax.rem(block + k, n_owners)
        pl.semaphore_signal(
            barrier, inc=1, device_id={"along": o // 2, "cross": lax.rem(o, 2)}, device_id_type=MESH
        )
        return carry

    lax.fori_loop(1, n_owners, greet, 0)

    for index, (src, dst) in enumerate(fields):
        if len(dst.shape) == 4:
            tail = PAD + ext + HALO
            dst[:, :, 0:PAD, :] = jnp.zeros((2, layers, PAD, cols), jnp.float32)
            dst[:, :, tail : tail + PAD, :] = jnp.zeros((2, layers, PAD, cols), jnp.float32)

    list_copy.wait()
    owner_copy.wait()
    patches = 2 * rows
    lane_r = lax.broadcasted_iota(jnp.int32, (patches, patches), 0)
    lane_c = lax.broadcasted_iota(jnp.int32, (patches, patches), 1)
    id_r = 2 * lax.rem(lane_r, rows) + lane_r // rows
    id_c = 2 * lax.rem(lane_c, rows) + lane_c // rows
    wanted = id_r + block * patches
    seen = jnp.zeros((patches, lists.shape[1]), jnp.float32)
    for row in range(lists.shape[0]):
        seen = jnp.where(lists[row : row + 1, :] == wanted, 1.0, seen)
    ones = jnp.ones((8, lists.shape[1]), jnp.bfloat16)
    member = lax.dot_general(
        ones, seen.astype(jnp.bfloat16), (((1,), (1,)), ((), ())), preferred_element_type=jnp.float32
    )
    permute = jnp.where(lane_r == id_c, 1.0, 0.0).astype(jnp.bfloat16)
    owner_rows = jnp.broadcast_to(owners[...].astype(jnp.float32), (8, patches)).astype(jnp.bfloat16)
    owner_of = jnp.dot(owner_rows, permute, preferred_element_type=jnp.float32)
    slot = lax.broadcasted_iota(jnp.int32, (slots, patches), 0)
    slot_owner = slot // cap
    slot_rank = (slot - slot_owner * cap).astype(jnp.float32)
    mine = owner_of[0:1, :] == slot_owner.astype(jnp.float32)
    before = jnp.where(id_r < id_c, 1.0, 0.0).astype(jnp.bfloat16)
    rank = jnp.dot(
        jnp.where(mine, 1.0, 0.0).astype(jnp.bfloat16), before, preferred_element_type=jnp.float32
    )
    held = jnp.where(mine & (rank == slot_rank), jnp.where(member[0:1, :] > 0.5, 1.0, 0.0), 0.0)
    place[...] = held.astype(jnp.bfloat16)

    pl.semaphore_wait(barrier, n_owners - 1)

    after_chip = lax.rem(i + 1, n_along)
    before_chip = lax.rem(i + n_along - 1, n_along)
    sends = []
    for index, (src, dst) in enumerate(fields):
        sends.append(
            pltpu.make_async_remote_copy(
                src_ref=take(src, rows - HALO, HALO),
                dst_ref=put(dst, j, PAD, HALO),
                send_sem=halo_send.at[index, 0],
                recv_sem=halo_recv.at[index, 1 + j],
                device_id={"along": after_chip, "cross": 0},
                device_id_type=MESH,
            )
        )
        sends.append(
            pltpu.make_async_remote_copy(
                src_ref=take(src, 0, HALO),
                dst_ref=put(dst, j, PAD + ext, HALO),
                send_sem=halo_send.at[index, 1],
                recv_sem=halo_recv.at[index, 1 + j],
                device_id={"along": before_chip, "cross": 1},
                device_id_type=MESH,
            )
        )
        sends.append(
            pltpu.make_async_remote_copy(
                src_ref=take(src, first_row(other), ext),
                dst_ref=put(dst, j, first_slot(other), ext),
                send_sem=halo_send.at[index, 2],
                recv_sem=halo_recv.at[index, 0],
                device_id={"cross": other},
                device_id_type=MESH,
            )
        )
    for copy in sends:
        copy.start()
    for copy in own_copies:
        copy.wait()
    for index, (src, dst) in enumerate(fields):
        for source in range(3):
            count = ext if source == 0 else HALO
            pltpu.make_async_copy(
                take(src, 0, count), put(dst, 0, PAD, count), halo_recv.at[index, source]
            ).wait()

    @pl.when((i == 0) & (j == 0))
    def _():
        ep[:, :, PAD : PAD + HALO, :] = jnp.zeros((2, layers, HALO, cols), jnp.float32)
        dx[:, PAD : PAD + HALO, :] = jnp.zeros((2, HALO, cols), jnp.int32)

    @pl.when((i == n_along - 1) & (j == 1))
    def _():
        ep[:, :, PAD + ext : PAD + ext + HALO, :] = jnp.zeros((2, layers, HALO, cols), jnp.float32)
        dx[:, PAD + ext : PAD + ext + HALO, :] = jnp.zeros((2, HALO, cols), jnp.int32)

    lane = lax.broadcasted_iota(jnp.int32, (8, cols), 1)
    first_lane = lane == 0
    last_lane = lane == cols - 1
    low_lanes = lax.broadcasted_iota(jnp.int32, (rows, cols), 1) < cols // 2
    zero = jnp.zeros((8, cols), jnp.float32)
    tiles = (half + 2 * HALO) // 8
    own_tiles = range(HALO // 8, HALO // 8 + half // 8)
    own_start = pl.multiple_of(half * j, 8)

    def trace_copy(t):
        return pltpu.make_async_remote_copy(
            src_ref=trace_out.at[t],
            dst_ref=trace.at[t, pl.ds(own_start, half), :],
            send_sem=trace_send.at[t],
            recv_sem=trace_recv.at[t],
            device_id={"cross": other},
            device_id_type=MESH,
        )

    def step(t):
        for tile in range(tiles):
            r = PAD + 8 * tile
            depth = [dx[h, r : r + 8, :] for h in range(2)]
            stiff = [kx[h, r : r + 8, :] for h in range(2)]
            half_stiff = [0.5 * stiff[h] for h in range(2)]
            for z in range(layers):
                pressure = [ep[h, z, r : r + 8, :] for h in range(2)]
                turned = [pltpu.roll(pressure[h], cols - 1, 1) for h in range(2)]
                right = [
                    jnp.where(last_lane, turned[1], turned[0]),
                    jnp.where(last_lane, 0.0, turned[1]),
                ]
                for h in range(2):
                    wet = depth[h] > z
                    ahead = ep[h, z, r + 1 : r + 9, :]
                    ea[h, z, r : r + 8, :] = jnp.where(
                        wet, ea[h, z, r : r + 8, :] - (ahead - pressure[h]), 0.0
                    )
                    ec[h, z, r : r + 8, :] = jnp.where(
                        wet, ec[h, z, r : r + 8, :] - (right[h] - pressure[h]), 0.0
                    )
            pressure = [ep[h, 0, r : r + 8, :] for h in range(2)]
            wet = [depth[h] > 0 for h in range(2)]
            down = [zero, zero]
            seafloor = [zero, zero]
            for z in range(layers):
                cross = [ec[h, z, r : r + 8, :] for h in range(2)]
                turned = [pltpu.roll(cross[h], 1, 1) for h in range(2)]
                left = [
                    jnp.where(first_lane, 0.0, turned[0]),
                    jnp.where(first_lane, turned[0], turned[1]),
                ]
                for h in range(2):
                    behind = ea[h, z, r - 1 : r + 7, :]
                    spread = (ea[h, z, r : r + 8, :] - behind) + (cross[h] - left[h])
                    if z + 1 < layers:
                        lower = ep[h, z + 1, r : r + 8, :]
                        wet_lower = depth[h] > z + 1
                        up = jnp.where(wet_lower, lower - pressure[h], 0.0)
                        vertical = up - down[h]
                    else:
                        vertical = -down[h]
                    value = pressure[h] - stiff[h] * spread + half_stiff[h] * vertical
                    value = jnp.where(wet[h], value, 0.0)
                    ep[h, z, r : r + 8, :] = value
                    seafloor[h] = jnp.where(wet[h], value, seafloor[h])
                    if z + 1 < layers:
                        pressure[h] = lower
                        wet[h] = wet_lower
                        down[h] = up
            if tile in own_tiles:
                at = 8 * (tile - HALO // 8)
                trace[t, pl.ds(pl.multiple_of(own_start + at, 8), 8), :] = jnp.where(
                    j == 0, seafloor[0], seafloor[1]
                )
                trace_out[t, at : at + 8, :] = jnp.where(j == 0, seafloor[1], seafloor[0])
        trace_copy(t).start()

    def panel_copy(g, k):
        o = lax.rem(block + k, n_owners)
        return pltpu.make_async_remote_copy(
            src_ref=outgoing.at[g, pl.ds(o * cap, cap)],
            dst_ref=out_s.at[pl.ds(block * cap, cap), g],
            send_sem=panel_send.at[g],
            recv_sem=panel_recv.at[g],
            device_id={"along": o // 2, "cross": lax.rem(o, 2)},
            device_id_type=MESH,
        )

    def own_panel_copy(g):
        return pltpu.make_async_copy(
            outgoing.at[g, pl.ds(block * cap, cap)],
            out_s.at[pl.ds(block * cap, cap), g],
            final_sem.at[2 + g],
        )

    def send_group(g):
        pair = []
        for s in range(2):
            trace_copy(2 * g + s).wait_recv()
        first, second = trace[2 * g], trace[2 * g + 1]
        left = jnp.where(low_lanes, first, pltpu.roll(second, cols // 2, 1))
        right = jnp.where(low_lanes, pltpu.roll(first, cols // 2, 1), second)
        rest = jnp.concatenate([left, right], 0)
        total = None
        for part in range(3):
            piece = rest.astype(jnp.bfloat16)
            term = jnp.dot(place[...], piece, preferred_element_type=jnp.float32)
            total = term if total is None else total + term
            rest = rest - piece.astype(jnp.float32)
        outgoing[g, :, 0, :] = total
        own_panel_copy(g).start()

        def send(k, carry):
            panel_copy(g, k).start()
            return carry

        lax.fori_loop(1, n_owners, send, 0)

    own_pressure = pltpu.make_async_copy(
        ep.at[j, :, pl.ds(PAD + HALO, half), :],
        out_p.at[0, :, pl.ds(own_start, half), :],
        final_sem.at[0],
    )
    other_pressure = pltpu.make_async_remote_copy(
        src_ref=ep.at[other, :, pl.ds(PAD + HALO, half), :],
        dst_ref=out_p.at[0, :, pl.ds(own_start, half), :],
        send_sem=final_sem.at[1],
        recv_sem=final_sem.at[6],
        device_id={"cross": other},
        device_id_type=MESH,
    )

    def advance(t, carry):
        @pl.when(t < STEPS)
        def _():
            step(t)

        @pl.when(t == STEPS - 1)
        def _():
            own_pressure.start()
            other_pressure.start()

        @pl.when((t >= 2) & (lax.rem(t, 2) == 0))
        def _():
            send_group(t // 2 - 1)

        return carry

    lax.fori_loop(0, STEPS + 1, advance, 0)

    for copy in sends:
        copy.wait_send()
    for t in range(STEPS):
        trace_copy(t).wait_send()
    own_pressure.wait()
    other_pressure.wait()
    moved = (n_owners - 1) * cap
    for g in range(STEPS // 2):
        own_panel_copy(g).wait()
        pltpu.make_async_copy(
            outgoing.at[g, pl.ds(0, moved)], out_s.at[pl.ds(0, moved), g], panel_send.at[g]
        ).wait()
        pltpu.make_async_copy(
            outgoing.at[g, pl.ds(0, moved)], out_s.at[pl.ds(0, moved), g], panel_recv.at[g]
        ).wait()


def shards(
    pressure_start, along_start, cross_start, depth_layers, stiffness, patch_lists, owner_map
):
    _, layers, rows, cols = pressure_start.shape
    n_along = lax.axis_size("along")
    n_owners = n_along * lax.axis_size("cross")
    cap = 2 * rows // n_owners + 1
    slots = n_owners * cap
    ext_rows = rows // 2 + 2 * HALO + 2 * PAD
    lists = patch_lists.reshape(-1, cols)
    any_space = pl.BlockSpec(memory_space=pl.ANY)
    pressure, panels = pl.pallas_call(
        functools.partial(kernel, n_along, layers, rows, cols, cap),
        out_shape=(
            jax.ShapeDtypeStruct(pressure_start.shape, jnp.float32),
            jax.ShapeDtypeStruct((slots, STEPS // 2, 1, cols), jnp.float32),
        ),
        in_specs=[any_space] * 7,
        out_specs=(any_space, any_space),
        scratch_shapes=[
            pltpu.VMEM((2, layers, ext_rows, cols), jnp.float32),
            pltpu.VMEM((2, layers, ext_rows, cols), jnp.float32),
            pltpu.VMEM((2, layers, ext_rows, cols), jnp.float32),
            pltpu.VMEM((2, ext_rows, cols), jnp.int32),
            pltpu.VMEM((2, ext_rows, cols), jnp.float32),
            pltpu.VMEM(lists.shape, jnp.int32),
            pltpu.VMEM(owner_map.shape, jnp.int32),
            pltpu.VMEM((slots, 2 * rows), jnp.bfloat16),
            pltpu.VMEM((STEPS, rows, cols), jnp.float32),
            pltpu.VMEM((STEPS, rows // 2, cols), jnp.float32),
            pltpu.VMEM((STEPS // 2, slots, 1, cols), jnp.float32),
            pltpu.SemaphoreType.DMA((7,)),
            pltpu.SemaphoreType.DMA((5, 3)),
            pltpu.SemaphoreType.DMA((5, 3)),
            pltpu.SemaphoreType.DMA((STEPS,)),
            pltpu.SemaphoreType.DMA((STEPS,)),
            pltpu.SemaphoreType.DMA((STEPS // 2,)),
            pltpu.SemaphoreType.DMA((STEPS // 2,)),
            pltpu.SemaphoreType.DMA((7,)),
        ],
        compiler_params=pltpu.CompilerParams(collective_id=0, has_side_effects=True),
    )(
        pressure_start,
        along_start,
        cross_start,
        depth_layers,
        stiffness,
        lists,
        owner_map,
    )
    return (pressure, panels.reshape(1, slots, 1, STEPS // 2 * cols))


def solution(mesh):
    in_specs = (
        P("batch", None, "along", "cross"),
        P("batch", None, "along", "cross"),
        P("batch", None, "along", "cross"),
        P("along", "cross"),
        P("along", "cross"),
        P("batch", None),
        P(("along", "cross"), None),
    )
    out_specs = (P("batch", None, "along", "cross"), P(("along", "cross"), None, "batch", None))
    return jax.shard_map(shards, mesh=mesh, in_specs=in_specs, out_specs=out_specs, check_vma=False)
```

```python
import functools

import jax
import jax.numpy as jnp
from jax import lax
from jax.experimental import pallas as pl
from jax.experimental.pallas import tpu as pltpu
from jax.sharding import PartitionSpec as P

STEPS = 8
HALO = 8
PAD = 8
MESH = pl.DeviceIdType.MESH


def kernel(
    n_along,
    layers,
    rows,
    cols,
    cap,
    p_hbm,
    fa_hbm,
    fc_hbm,
    d_hbm,
    k_hbm,
    lists_hbm,
    owners_hbm,
    out_p,
    out_s,
    ep,
    ea,
    ec,
    dx,
    kx,
    lists,
    owners,
    place,
    trace,
    trace_out,
    outgoing,
    local_sem,
    halo_send,
    halo_recv,
    trace_send,
    trace_recv,
    panel_send,
    panel_recv,
    final_sem,
    round_sem,
):
    i = lax.axis_index("along")
    j = lax.axis_index("cross")
    other = 1 - j
    block = i * 2 + j
    n_owners = 2 * n_along
    half = rows // 2
    ext = half + HALO
    slots = n_owners * cap

    list_copy = pltpu.make_async_copy(lists_hbm, lists, local_sem.at[5])
    owner_copy = pltpu.make_async_copy(owners_hbm, owners, local_sem.at[6])
    list_copy.start()
    owner_copy.start()
    fields = ((p_hbm, ep), (fa_hbm, ea), (fc_hbm, ec), (d_hbm, dx), (k_hbm, kx))

    def take(src, start, count):
        if len(src.shape) == 4:
            return src.at[0, :, pl.ds(start, count), :]
        return src.at[pl.ds(start, count), :]

    def put(dst, side, start, count):
        if len(dst.shape) == 4:
            return dst.at[side, :, pl.ds(start, count), :]
        return dst.at[side, pl.ds(start, count), :]

    def first_row(core):
        return pl.multiple_of((half - HALO) * core, 8)

    def first_slot(core):
        return pl.multiple_of(PAD + HALO - HALO * core, 8)

    own_copies = []
    for index, (src, dst) in enumerate(fields):
        copy = pltpu.make_async_copy(
            take(src, first_row(j), ext), put(dst, j, first_slot(j), ext), local_sem.at[index]
        )
        copy.start()
        own_copies.append(copy)

    after_chip = lax.rem(i + 1, n_along)
    before_chip = lax.rem(i + n_along - 1, n_along)
    barrier = pltpu.get_barrier_semaphore()
    pl.semaphore_signal(barrier, inc=1, device_id={"cross": other}, device_id_type=MESH)
    for chip in (after_chip, before_chip):
        for core in range(2):
            pl.semaphore_signal(
                barrier, inc=1, device_id={"along": chip, "cross": core}, device_id_type=MESH
            )

    for index, (src, dst) in enumerate(fields):
        if len(dst.shape) == 4:
            tail = PAD + ext + HALO
            dst[:, :, 0:PAD, :] = jnp.zeros((2, layers, PAD, cols), jnp.float32)
            dst[:, :, tail : tail + PAD, :] = jnp.zeros((2, layers, PAD, cols), jnp.float32)

    list_copy.wait()
    owner_copy.wait()
    patches = 2 * rows
    lane_r = lax.broadcasted_iota(jnp.int32, (patches, patches), 0)
    lane_c = lax.broadcasted_iota(jnp.int32, (patches, patches), 1)
    id_r = 2 * lax.rem(lane_r, rows) + lane_r // rows
    id_c = 2 * lax.rem(lane_c, rows) + lane_c // rows
    wanted = id_r + block * patches
    seen = jnp.zeros((patches, lists.shape[1]), jnp.float32)
    for row in range(lists.shape[0]):
        seen = jnp.where(lists[row : row + 1, :] == wanted, 1.0, seen)
    ones = jnp.ones((8, lists.shape[1]), jnp.bfloat16)
    member = lax.dot_general(
        ones, seen.astype(jnp.bfloat16), (((1,), (1,)), ((), ())), preferred_element_type=jnp.float32
    )
    permute = jnp.where(lane_r == id_c, 1.0, 0.0).astype(jnp.bfloat16)
    owner_rows = jnp.broadcast_to(owners[...].astype(jnp.float32), (8, patches)).astype(jnp.bfloat16)
    owner_of = jnp.dot(owner_rows, permute, preferred_element_type=jnp.float32)
    slot = lax.broadcasted_iota(jnp.int32, (slots, patches), 0)
    slot_owner = slot // cap
    slot_rank = (slot - slot_owner * cap).astype(jnp.float32)
    mine = owner_of[0:1, :] == slot_owner.astype(jnp.float32)
    before = jnp.where(id_r < id_c, 1.0, 0.0).astype(jnp.bfloat16)
    rank = jnp.dot(
        jnp.where(mine, 1.0, 0.0).astype(jnp.bfloat16), before, preferred_element_type=jnp.float32
    )
    held = jnp.where(mine & (rank == slot_rank), jnp.where(member[0:1, :] > 0.5, 1.0, 0.0), 0.0)
    place[...] = held.astype(jnp.bfloat16)

    pl.semaphore_wait(barrier, 5)

    sends = []
    for index, (src, dst) in enumerate(fields):
        sends.append(
            pltpu.make_async_remote_copy(
                src_ref=take(src, rows - HALO, HALO),
                dst_ref=put(dst, j, PAD, HALO),
                send_sem=halo_send.at[index, 0],
                recv_sem=halo_recv.at[index, 1 + j],
                device_id={"along": after_chip, "cross": 0},
                device_id_type=MESH,
            )
        )
        sends.append(
            pltpu.make_async_remote_copy(
                src_ref=take(src, 0, HALO),
                dst_ref=put(dst, j, PAD + ext, HALO),
                send_sem=halo_send.at[index, 1],
                recv_sem=halo_recv.at[index, 1 + j],
                device_id={"along": before_chip, "cross": 1},
                device_id_type=MESH,
            )
        )
        sends.append(
            pltpu.make_async_remote_copy(
                src_ref=take(src, first_row(other), ext),
                dst_ref=put(dst, j, first_slot(other), ext),
                send_sem=halo_send.at[index, 2],
                recv_sem=halo_recv.at[index, 0],
                device_id={"cross": other},
                device_id_type=MESH,
            )
        )
    for copy in sends[0::3] + sends[1::3] + sends[2::3]:
        copy.start()

    reach = 1
    while reach < n_along // 2:
        for away in (reach, n_along - reach):
            pl.semaphore_signal(
                round_sem.at[reach.bit_length() - 1],
                inc=1,
                device_id={"along": lax.rem(i + away, n_along)},
                device_id_type=MESH,
            )
        pl.semaphore_wait(round_sem.at[reach.bit_length() - 1], 2)
        reach *= 2

    for copy in own_copies:
        copy.wait()
    for index, (src, dst) in enumerate(fields):
        for source in range(3):
            count = ext if source == 0 else HALO
            pltpu.make_async_copy(
                take(src, 0, count), put(dst, 0, PAD, count), halo_recv.at[index, source]
            ).wait()

    @pl.when((i == 0) & (j == 0))
    def _():
        ep[:, :, PAD : PAD + HALO, :] = jnp.zeros((2, layers, HALO, cols), jnp.float32)
        dx[:, PAD : PAD + HALO, :] = jnp.zeros((2, HALO, cols), jnp.int32)

    @pl.when((i == n_along - 1) & (j == 1))
    def _():
        ep[:, :, PAD + ext : PAD + ext + HALO, :] = jnp.zeros((2, layers, HALO, cols), jnp.float32)
        dx[:, PAD + ext : PAD + ext + HALO, :] = jnp.zeros((2, HALO, cols), jnp.int32)

    lane = lax.broadcasted_iota(jnp.int32, (8, cols), 1)
    first_lane = lane == 0
    last_lane = lane == cols - 1
    low_lanes = lax.broadcasted_iota(jnp.int32, (rows, cols), 1) < cols // 2
    zero = jnp.zeros((8, cols), jnp.float32)
    tiles = (half + 2 * HALO) // 8
    own_tiles = range(HALO // 8, HALO // 8 + half // 8)
    own_start = pl.multiple_of(half * j, 8)

    def trace_copy(t):
        return pltpu.make_async_remote_copy(
            src_ref=trace_out.at[t],
            dst_ref=trace.at[t, pl.ds(own_start, half), :],
            send_sem=trace_send.at[t],
            recv_sem=trace_recv.at[t],
            device_id={"cross": other},
            device_id_type=MESH,
        )

    def step(t, between=()):
        share = -(-len(between) // tiles)
        for tile in range(tiles):
            r = PAD + 8 * tile
            depth = [dx[h, r : r + 8, :] for h in range(2)]
            stiff = [kx[h, r : r + 8, :] for h in range(2)]
            half_stiff = [0.5 * stiff[h] for h in range(2)]
            for z in range(layers):
                pressure = [ep[h, z, r : r + 8, :] for h in range(2)]
                turned = [pltpu.roll(pressure[h], cols - 1, 1) for h in range(2)]
                right = [
                    jnp.where(last_lane, turned[1], turned[0]),
                    jnp.where(last_lane, 0.0, turned[1]),
                ]
                for h in range(2):
                    wet = depth[h] > z
                    ahead = ep[h, z, r + 1 : r + 9, :]
                    ea[h, z, r : r + 8, :] = jnp.where(
                        wet, ea[h, z, r : r + 8, :] - (ahead - pressure[h]), 0.0
                    )
                    ec[h, z, r : r + 8, :] = jnp.where(
                        wet, ec[h, z, r : r + 8, :] - (right[h] - pressure[h]), 0.0
                    )
            pressure = [ep[h, 0, r : r + 8, :] for h in range(2)]
            wet = [depth[h] > 0 for h in range(2)]
            down = [zero, zero]
            seafloor = [zero, zero]
            for z in range(layers):
                cross = [ec[h, z, r : r + 8, :] for h in range(2)]
                turned = [pltpu.roll(cross[h], 1, 1) for h in range(2)]
                left = [
                    jnp.where(first_lane, 0.0, turned[0]),
                    jnp.where(first_lane, turned[0], turned[1]),
                ]
                for h in range(2):
                    behind = ea[h, z, r - 1 : r + 7, :]
                    spread = (ea[h, z, r : r + 8, :] - behind) + (cross[h] - left[h])
                    if z + 1 < layers:
                        lower = ep[h, z + 1, r : r + 8, :]
                        wet_lower = depth[h] > z + 1
                        up = jnp.where(wet_lower, lower - pressure[h], 0.0)
                        vertical = up - down[h]
                    else:
                        vertical = -down[h]
                    value = pressure[h] - stiff[h] * spread + half_stiff[h] * vertical
                    value = jnp.where(wet[h], value, 0.0)
                    ep[h, z, r : r + 8, :] = value
                    seafloor[h] = jnp.where(wet[h], value, seafloor[h])
                    if z + 1 < layers:
                        pressure[h] = lower
                        wet[h] = wet_lower
                        down[h] = up
            for emit in between[share * tile : share * (tile + 1)]:
                emit()
            if tile in own_tiles:
                at = 8 * (tile - HALO // 8)
                trace[t, pl.ds(pl.multiple_of(own_start + at, 8), 8), :] = jnp.where(
                    j == 0, seafloor[0], seafloor[1]
                )
                trace_out[t, at : at + 8, :] = jnp.where(j == 0, seafloor[1], seafloor[0])
        trace_copy(t).start()

    order = []
    for away in range(n_along // 2, 0, -1):
        order += [away] if away == n_along // 2 else [away, n_along - away]
    targets = [(lax.rem(i + away, n_along), core) for away in order for core in (j, other)]
    targets.append((i, other))

    def panel_copy(g, target):
        chip, core = target
        return pltpu.make_async_remote_copy(
            src_ref=outgoing.at[g, pl.ds((2 * chip + core) * cap, cap)],
            dst_ref=out_s.at[pl.ds(block * cap, cap), g],
            send_sem=panel_send.at[g],
            recv_sem=panel_recv.at[g],
            device_id={"along": chip, "cross": core},
            device_id_type=MESH,
        )

    def own_panel_copy(g):
        return pltpu.make_async_copy(
            outgoing.at[g, pl.ds(block * cap, cap)],
            out_s.at[pl.ds(block * cap, cap), g],
            final_sem.at[2 + g],
        )

    def fill_group(g):
        for s in range(2):
            trace_copy(2 * g + s).wait_recv()
        first, second = trace[2 * g], trace[2 * g + 1]
        left = jnp.where(low_lanes, first, pltpu.roll(second, cols // 2, 1))
        right = jnp.where(low_lanes, pltpu.roll(first, cols // 2, 1), second)
        rest = jnp.concatenate([left, right], 0)
        total = None
        for part in range(3):
            piece = rest.astype(jnp.bfloat16)
            term = jnp.dot(place[...], piece, preferred_element_type=jnp.float32)
            total = term if total is None else total + term
            rest = rest - piece.astype(jnp.float32)
        outgoing[g, :, 0, :] = total
        own_panel_copy(g).start()

    def group_sends(g):
        return [functools.partial(lambda target: panel_copy(g, target).start(), t) for t in targets]

    own_pressure = pltpu.make_async_copy(
        ep.at[j, :, pl.ds(PAD + HALO, half), :],
        out_p.at[0, :, pl.ds(own_start, half), :],
        final_sem.at[0],
    )
    other_pressure = pltpu.make_async_remote_copy(
        src_ref=ep.at[other, :, pl.ds(PAD + HALO, half), :],
        dst_ref=out_p.at[0, :, pl.ds(own_start, half), :],
        send_sem=final_sem.at[1],
        recv_sem=final_sem.at[6],
        device_id={"cross": other},
        device_id_type=MESH,
    )

    def first_steps(t, carry):
        step(t)
        return carry

    def advance(g, carry):
        step(2 * g + 2)
        fill_group(g)
        step(2 * g + 3, group_sends(g))
        return carry

    groups = STEPS // 2
    lax.fori_loop(0, 2, first_steps, 0)
    lax.fori_loop(0, groups - 1, advance, 0)
    own_pressure.start()
    other_pressure.start()
    fill_group(groups - 1)
    for emit in group_sends(groups - 1):
        emit()

    for copy in sends:
        copy.wait_send()
    for t in range(STEPS):
        trace_copy(t).wait_send()
    own_pressure.wait()
    other_pressure.wait()
    moved = (n_owners - 1) * cap
    for g in range(STEPS // 2):
        own_panel_copy(g).wait()
        pltpu.make_async_copy(
            outgoing.at[g, pl.ds(0, moved)], out_s.at[pl.ds(0, moved), g], panel_send.at[g]
        ).wait()
        pltpu.make_async_copy(
            outgoing.at[g, pl.ds(0, moved)], out_s.at[pl.ds(0, moved), g], panel_recv.at[g]
        ).wait()


def shards(
    pressure_start, along_start, cross_start, depth_layers, stiffness, patch_lists, owner_map
):
    _, layers, rows, cols = pressure_start.shape
    n_along = lax.axis_size("along")
    n_owners = n_along * lax.axis_size("cross")
    cap = 2 * rows // n_owners + 1
    slots = n_owners * cap
    ext_rows = rows // 2 + 2 * HALO + 2 * PAD
    lists = patch_lists.reshape(-1, cols)
    any_space = pl.BlockSpec(memory_space=pl.ANY)
    pressure, panels = pl.pallas_call(
        functools.partial(kernel, n_along, layers, rows, cols, cap),
        out_shape=(
            jax.ShapeDtypeStruct(pressure_start.shape, jnp.float32),
            jax.ShapeDtypeStruct((slots, STEPS // 2, 1, cols), jnp.float32),
        ),
        in_specs=[any_space] * 7,
        out_specs=(any_space, any_space),
        scratch_shapes=[
            pltpu.VMEM((2, layers, ext_rows, cols), jnp.float32),
            pltpu.VMEM((2, layers, ext_rows, cols), jnp.float32),
            pltpu.VMEM((2, layers, ext_rows, cols), jnp.float32),
            pltpu.VMEM((2, ext_rows, cols), jnp.int32),
            pltpu.VMEM((2, ext_rows, cols), jnp.float32),
            pltpu.VMEM(lists.shape, jnp.int32),
            pltpu.VMEM(owner_map.shape, jnp.int32),
            pltpu.VMEM((slots, 2 * rows), jnp.bfloat16),
            pltpu.VMEM((STEPS, rows, cols), jnp.float32),
            pltpu.VMEM((STEPS, rows // 2, cols), jnp.float32),
            pltpu.VMEM((STEPS // 2, slots, 1, cols), jnp.float32),
            pltpu.SemaphoreType.DMA((7,)),
            pltpu.SemaphoreType.DMA((5, 3)),
            pltpu.SemaphoreType.DMA((5, 3)),
            pltpu.SemaphoreType.DMA((STEPS,)),
            pltpu.SemaphoreType.DMA((STEPS,)),
            pltpu.SemaphoreType.DMA((STEPS // 2,)),
            pltpu.SemaphoreType.DMA((STEPS // 2,)),
            pltpu.SemaphoreType.DMA((7,)),
            pltpu.SemaphoreType.REGULAR((max(1, n_along.bit_length() - 2),)),
        ],
        compiler_params=pltpu.CompilerParams(collective_id=0, has_side_effects=True),
    )(
        pressure_start,
        along_start,
        cross_start,
        depth_layers,
        stiffness,
        lists,
        owner_map,
    )
    return (pressure, panels.reshape(1, slots, 1, STEPS // 2 * cols))


def solution(mesh):
    in_specs = (
        P("batch", None, "along", "cross"),
        P("batch", None, "along", "cross"),
        P("batch", None, "along", "cross"),
        P("along", "cross"),
        P("along", "cross"),
        P("batch", None),
        P(("along", "cross"), None),
    )
    out_specs = (P("batch", None, "along", "cross"), P(("along", "cross"), None, "batch", None))
    return jax.shard_map(shards, mesh=mesh, in_specs=in_specs, out_specs=out_specs, check_vma=False)
```

```python
import functools

import jax
import jax.numpy as jnp
from jax import lax
from jax.experimental import pallas as pl
from jax.experimental.pallas import tpu as pltpu
from jax.sharding import PartitionSpec as P

STEPS = 8
HALO = 8
PAD = 8
LAG = 3
MESH = pl.DeviceIdType.MESH


def kernel(
    n_along,
    layers,
    rows,
    cols,
    cap,
    p_hbm,
    fa_hbm,
    fc_hbm,
    d_hbm,
    k_hbm,
    lists_hbm,
    owners_hbm,
    out_p,
    out_s,
    ep,
    ea,
    ec,
    dx,
    kx,
    lists,
    owners,
    place,
    trace,
    trace_out,
    outgoing,
    local_sem,
    halo_send,
    halo_recv,
    trace_send,
    trace_recv,
    panel_send,
    panel_recv,
    final_sem,
    round_sem,
    landed,
    store_sem,
):
    i = lax.axis_index("along")
    j = lax.axis_index("cross")
    other = 1 - j
    block = i * 2 + j
    n_owners = 2 * n_along
    half = rows // 2
    ext = half + HALO
    slots = n_owners * cap

    list_copy = pltpu.make_async_copy(lists_hbm, lists, local_sem.at[5])
    owner_copy = pltpu.make_async_copy(owners_hbm, owners, local_sem.at[6])
    list_copy.start()
    owner_copy.start()
    fields = ((p_hbm, ep), (fa_hbm, ea), (fc_hbm, ec), (d_hbm, dx), (k_hbm, kx))

    def take(src, start, count):
        if len(src.shape) == 4:
            return src.at[0, :, pl.ds(start, count), :]
        return src.at[pl.ds(start, count), :]

    def put(dst, side, start, count):
        if len(dst.shape) == 4:
            return dst.at[side, :, pl.ds(start, count), :]
        return dst.at[side, pl.ds(start, count), :]

    def first_row(core):
        return pl.multiple_of((half - HALO) * core, 8)

    def first_slot(core):
        return pl.multiple_of(PAD + HALO - HALO * core, 8)

    own_copies = []
    for index, (src, dst) in enumerate(fields):
        copy = pltpu.make_async_copy(
            take(src, first_row(j), ext), put(dst, j, first_slot(j), ext), local_sem.at[index]
        )
        copy.start()
        own_copies.append(copy)

    after_chip = lax.rem(i + 1, n_along)
    before_chip = lax.rem(i + n_along - 1, n_along)
    barrier = pltpu.get_barrier_semaphore()
    pl.semaphore_signal(barrier, inc=1, device_id={"cross": other}, device_id_type=MESH)
    for chip in (after_chip, before_chip):
        for core in range(2):
            pl.semaphore_signal(
                barrier, inc=1, device_id={"along": chip, "cross": core}, device_id_type=MESH
            )

    for index, (src, dst) in enumerate(fields):
        if len(dst.shape) == 4:
            tail = PAD + ext + HALO
            dst[:, :, 0:PAD, :] = jnp.zeros((2, layers, PAD, cols), jnp.float32)
            dst[:, :, tail : tail + PAD, :] = jnp.zeros((2, layers, PAD, cols), jnp.float32)

    list_copy.wait()
    owner_copy.wait()
    patches = 2 * rows
    lane_r = lax.broadcasted_iota(jnp.int32, (patches, patches), 0)
    lane_c = lax.broadcasted_iota(jnp.int32, (patches, patches), 1)
    id_r = 2 * lax.rem(lane_r, rows) + lane_r // rows
    id_c = 2 * lax.rem(lane_c, rows) + lane_c // rows
    wanted = id_r + block * patches
    seen = jnp.zeros((patches, lists.shape[1]), jnp.float32)
    for row in range(lists.shape[0]):
        seen = jnp.where(lists[row : row + 1, :] == wanted, 1.0, seen)
    ones = jnp.ones((8, lists.shape[1]), jnp.bfloat16)
    member = lax.dot_general(
        ones, seen.astype(jnp.bfloat16), (((1,), (1,)), ((), ())), preferred_element_type=jnp.float32
    )
    permute = jnp.where(lane_r == id_c, 1.0, 0.0).astype(jnp.bfloat16)
    owner_rows = jnp.broadcast_to(owners[...].astype(jnp.float32), (8, patches)).astype(jnp.bfloat16)
    owner_of = jnp.dot(owner_rows, permute, preferred_element_type=jnp.float32)
    slot = lax.broadcasted_iota(jnp.int32, (slots, patches), 0)
    slot_owner = slot // cap
    slot_rank = (slot - slot_owner * cap).astype(jnp.float32)
    mine = owner_of[0:1, :] == slot_owner.astype(jnp.float32)
    before = jnp.where(id_r < id_c, 1.0, 0.0).astype(jnp.bfloat16)
    rank = jnp.dot(
        jnp.where(mine, 1.0, 0.0).astype(jnp.bfloat16), before, preferred_element_type=jnp.float32
    )
    held = jnp.where(mine & (rank == slot_rank), jnp.where(member[0:1, :] > 0.5, 1.0, 0.0), 0.0)
    place[...] = held.astype(jnp.bfloat16)

    pl.semaphore_wait(barrier, 5)

    sends = []
    for index, (src, dst) in enumerate(fields):
        sends.append(
            pltpu.make_async_remote_copy(
                src_ref=take(src, rows - HALO, HALO),
                dst_ref=put(dst, j, PAD, HALO),
                send_sem=halo_send.at[index, 0],
                recv_sem=halo_recv.at[index, 1 + j],
                device_id={"along": after_chip, "cross": 0},
                device_id_type=MESH,
            )
        )
        sends.append(
            pltpu.make_async_remote_copy(
                src_ref=take(src, 0, HALO),
                dst_ref=put(dst, j, PAD + ext, HALO),
                send_sem=halo_send.at[index, 1],
                recv_sem=halo_recv.at[index, 1 + j],
                device_id={"along": before_chip, "cross": 1},
                device_id_type=MESH,
            )
        )
        sends.append(
            pltpu.make_async_remote_copy(
                src_ref=take(src, first_row(other), ext),
                dst_ref=put(dst, j, first_slot(other), ext),
                send_sem=halo_send.at[index, 2],
                recv_sem=halo_recv.at[index, 0],
                device_id={"cross": other},
                device_id_type=MESH,
            )
        )
    for copy in sends[0::3] + sends[1::3] + sends[2::3]:
        copy.start()

    rounds = max(1, n_along.bit_length() - 2)

    def tell(index):
        for away in (1 << index, n_along - (1 << index)):
            pl.semaphore_signal(
                round_sem.at[index],
                inc=1,
                device_id={"along": lax.rem(i + away, n_along)},
                device_id_type=MESH,
            )

    for index in range(rounds):
        tell(index)
        if index + 1 < rounds:
            pl.semaphore_wait(round_sem.at[index], 2)

    for copy in own_copies:
        copy.wait()
    for index, (src, dst) in enumerate(fields):
        for source in range(3):
            count = ext if source == 0 else HALO
            pltpu.make_async_copy(
                take(src, 0, count), put(dst, 0, PAD, count), halo_recv.at[index, source]
            ).wait()

    @pl.when((i == 0) & (j == 0))
    def _():
        ep[:, :, PAD : PAD + HALO, :] = jnp.zeros((2, layers, HALO, cols), jnp.float32)
        dx[:, PAD : PAD + HALO, :] = jnp.zeros((2, HALO, cols), jnp.int32)

    @pl.when((i == n_along - 1) & (j == 1))
    def _():
        ep[:, :, PAD + ext : PAD + ext + HALO, :] = jnp.zeros((2, layers, HALO, cols), jnp.float32)
        dx[:, PAD + ext : PAD + ext + HALO, :] = jnp.zeros((2, HALO, cols), jnp.int32)

    lane = lax.broadcasted_iota(jnp.int32, (8, cols), 1)
    first_lane = lane == 0
    last_lane = lane == cols - 1
    low_lanes = lax.broadcasted_iota(jnp.int32, (rows, cols), 1) < cols // 2
    zero = jnp.zeros((8, cols), jnp.float32)
    tiles = (half + 2 * HALO) // 8
    own_tiles = range(HALO // 8, HALO // 8 + half // 8)
    own_start = pl.multiple_of(half * j, 8)

    def trace_copy(t):
        return pltpu.make_async_remote_copy(
            src_ref=trace_out.at[t],
            dst_ref=trace.at[t, pl.ds(own_start, half), :],
            send_sem=trace_send.at[t],
            recv_sem=trace_recv.at[t],
            device_id={"cross": other},
            device_id_type=MESH,
        )

    def step(t, between=()):
        share = -(-len(between) // tiles)

        def rows_of(tile):
            r = PAD + 8 * tile
            return r, slice(r, r + 8)

        def flows(tile):
            r, at = rows_of(tile)
            depth = [dx[h, at, :] for h in range(2)]
            ready = {}
            for tick in range(layers + LAG):
                if tick < layers:
                    pressure = [ep[h, tick, at, :] for h in range(2)]
                    ready[tick] = (
                        pressure,
                        [pltpu.roll(pressure[h], cols - 1, 1) for h in range(2)],
                    )
                z = tick - LAG
                if z >= 0:
                    pressure, turned = ready.pop(z)
                    right = [
                        jnp.where(last_lane, turned[1], turned[0]),
                        jnp.where(last_lane, 0.0, turned[1]),
                    ]
                    for h in range(2):
                        wet = depth[h] > z
                        ahead = ep[h, z, r + 1 : r + 9, :]
                        ea[h, z, at, :] = jnp.where(
                            wet, ea[h, z, at, :] - (ahead - pressure[h]), 0.0
                        )
                        ec[h, z, at, :] = jnp.where(
                            wet, ec[h, z, at, :] - (right[h] - pressure[h]), 0.0
                        )
                yield

        def pressures(tile):
            r, at = rows_of(tile)
            depth = [dx[h, at, :] for h in range(2)]
            stiff = [kx[h, at, :] for h in range(2)]
            half_stiff = [0.5 * stiff[h] for h in range(2)]
            pressure = [ep[h, 0, at, :] for h in range(2)]
            wet = [depth[h] > 0 for h in range(2)]
            down = [zero, zero]
            seafloor = [zero, zero]
            ready = {}
            for tick in range(layers + LAG):
                if tick < layers:
                    cross = [ec[h, tick, at, :] for h in range(2)]
                    ready[tick] = (cross, [pltpu.roll(cross[h], 1, 1) for h in range(2)])
                z = tick - LAG
                if z >= 0:
                    cross, turned = ready.pop(z)
                    left = [
                        jnp.where(first_lane, 0.0, turned[0]),
                        jnp.where(first_lane, turned[0], turned[1]),
                    ]
                    for h in range(2):
                        spread = (ea[h, z, at, :] - ea[h, z, r - 1 : r + 7, :]) + (
                            cross[h] - left[h]
                        )
                        if z + 1 < layers:
                            lower = ep[h, z + 1, at, :]
                            wet_lower = depth[h] > z + 1
                            up = jnp.where(wet_lower, lower - pressure[h], 0.0)
                            vertical = up - down[h]
                        else:
                            vertical = -down[h]
                        value = pressure[h] - stiff[h] * spread + half_stiff[h] * vertical
                        value = jnp.where(wet[h], value, 0.0)
                        ep[h, z, at, :] = value
                        if tile in own_tiles:
                            seafloor[h] = jnp.where(wet[h], value, seafloor[h])
                        if z + 1 < layers:
                            pressure[h], wet[h], down[h] = lower, wet_lower, up
                yield
            if tile in own_tiles:
                to = 8 * (tile - HALO // 8)
                trace[t, pl.ds(pl.multiple_of(own_start + to, 8), 8), :] = jnp.where(
                    j == 0, seafloor[0], seafloor[1]
                )
                trace_out[t, to : to + 8, :] = jnp.where(j == 0, seafloor[1], seafloor[0])

        for tile in range(tiles + 1):
            work = []
            if tile < tiles:
                work.append(flows(tile))
            if tile > 0:
                work.append(pressures(tile - 1))
            for _ in range(layers + LAG + 1):
                for part in work:
                    next(part, None)
            if tile < tiles:
                for emit in between[share * tile : share * (tile + 1)]:
                    emit()
        trace_copy(t).start()

    order = []
    for away in range(n_along // 2, 0, -1):
        order += [away] if away == n_along // 2 else [away, n_along - away]
    targets = [(lax.rem(i + away, n_along), core) for away in order for core in (j, other)]
    targets.append((i, other))

    def panel_copy(g, target):
        chip, core = target
        return pltpu.make_async_remote_copy(
            src_ref=outgoing.at[g, pl.ds((2 * chip + core) * cap, cap)],
            dst_ref=landed.at[g, pl.ds(block * cap, cap)],
            send_sem=panel_send.at[g],
            recv_sem=panel_recv.at[g],
            device_id={"along": chip, "cross": core},
            device_id_type=MESH,
        )

    def own_panel_copy(g):
        return pltpu.make_async_copy(
            outgoing.at[g, pl.ds(block * cap, cap)],
            landed.at[g, pl.ds(block * cap, cap)],
            final_sem.at[2 + g],
        )

    def fill_group(g):
        for s in range(2):
            trace_copy(2 * g + s).wait_recv()
        first, second = trace[2 * g], trace[2 * g + 1]
        left = jnp.where(low_lanes, first, pltpu.roll(second, cols // 2, 1))
        right = jnp.where(low_lanes, pltpu.roll(first, cols // 2, 1), second)
        rest = jnp.concatenate([left, right], 0)
        total = None
        for part in range(3):
            piece = rest.astype(jnp.bfloat16)
            term = jnp.dot(place[...], piece, preferred_element_type=jnp.float32)
            total = term if total is None else total + term
            rest = rest - piece.astype(jnp.float32)
        outgoing[g, :, 0, :] = total
        own_panel_copy(g).start()

    def group_sends(g):
        return [functools.partial(lambda target: panel_copy(g, target).start(), t) for t in targets]

    own_pressure = pltpu.make_async_copy(
        ep.at[j, :, pl.ds(PAD + HALO, half), :],
        out_p.at[0, :, pl.ds(own_start, half), :],
        final_sem.at[0],
    )
    other_pressure = pltpu.make_async_remote_copy(
        src_ref=ep.at[other, :, pl.ds(PAD + HALO, half), :],
        dst_ref=out_p.at[0, :, pl.ds(own_start, half), :],
        send_sem=final_sem.at[1],
        recv_sem=final_sem.at[6],
        device_id={"cross": other},
        device_id_type=MESH,
    )

    def first_steps(t, carry):
        step(t)
        return carry

    def advance(g, carry):
        step(2 * g + 2)
        fill_group(g)
        step(2 * g + 3, group_sends(g))
        return carry

    groups = STEPS // 2
    lax.fori_loop(0, 2, first_steps, 0)
    pl.semaphore_wait(round_sem.at[rounds - 1], 2)
    lax.fori_loop(0, groups - 1, advance, 0)
    own_pressure.start()
    other_pressure.start()
    fill_group(groups - 1)
    for emit in group_sends(groups - 1):
        emit()

    for copy in sends:
        copy.wait_send()
    for t in range(STEPS):
        trace_copy(t).wait_send()
    own_pressure.wait()
    other_pressure.wait()
    moved = (n_owners - 1) * cap
    stores = []
    for g in range(groups):
        own_panel_copy(g).wait()
        pltpu.make_async_copy(
            outgoing.at[g, pl.ds(0, moved)], landed.at[g, pl.ds(0, moved)], panel_recv.at[g]
        ).wait()
        copy = pltpu.make_async_copy(landed.at[g], out_s.at[:, g], store_sem.at[g])
        copy.start()
        stores.append(copy)
    for g in range(groups):
        pltpu.make_async_copy(
            outgoing.at[g, pl.ds(0, moved)], landed.at[g, pl.ds(0, moved)], panel_send.at[g]
        ).wait()
    for copy in stores:
        copy.wait()


def shards(
    pressure_start, along_start, cross_start, depth_layers, stiffness, patch_lists, owner_map
):
    _, layers, rows, cols = pressure_start.shape
    n_along = lax.axis_size("along")
    n_owners = n_along * lax.axis_size("cross")
    cap = 2 * rows // n_owners + 1
    slots = n_owners * cap
    ext_rows = rows // 2 + 2 * HALO + 2 * PAD
    lists = patch_lists.reshape(-1, cols)
    any_space = pl.BlockSpec(memory_space=pl.ANY)
    pressure, panels = pl.pallas_call(
        functools.partial(kernel, n_along, layers, rows, cols, cap),
        out_shape=(
            jax.ShapeDtypeStruct(pressure_start.shape, jnp.float32),
            jax.ShapeDtypeStruct((slots, STEPS // 2, 1, cols), jnp.float32),
        ),
        in_specs=[any_space] * 7,
        out_specs=(any_space, any_space),
        scratch_shapes=[
            pltpu.VMEM((2, layers, ext_rows, cols), jnp.float32),
            pltpu.VMEM((2, layers, ext_rows, cols), jnp.float32),
            pltpu.VMEM((2, layers, ext_rows, cols), jnp.float32),
            pltpu.VMEM((2, ext_rows, cols), jnp.int32),
            pltpu.VMEM((2, ext_rows, cols), jnp.float32),
            pltpu.VMEM(lists.shape, jnp.int32),
            pltpu.VMEM(owner_map.shape, jnp.int32),
            pltpu.VMEM((slots, 2 * rows), jnp.bfloat16),
            pltpu.VMEM((STEPS, rows, cols), jnp.float32),
            pltpu.VMEM((STEPS, rows // 2, cols), jnp.float32),
            pltpu.VMEM((STEPS // 2, slots, 1, cols), jnp.float32),
            pltpu.SemaphoreType.DMA((7,)),
            pltpu.SemaphoreType.DMA((5, 3)),
            pltpu.SemaphoreType.DMA((5, 3)),
            pltpu.SemaphoreType.DMA((STEPS,)),
            pltpu.SemaphoreType.DMA((STEPS,)),
            pltpu.SemaphoreType.DMA((STEPS // 2,)),
            pltpu.SemaphoreType.DMA((STEPS // 2,)),
            pltpu.SemaphoreType.DMA((7,)),
            pltpu.SemaphoreType.REGULAR((max(1, n_along.bit_length() - 2),)),
            pltpu.VMEM((STEPS // 2, slots, 1, cols), jnp.float32),
            pltpu.SemaphoreType.DMA((STEPS // 2,)),
        ],
        compiler_params=pltpu.CompilerParams(collective_id=0, has_side_effects=True, vmem_limit_bytes=16 << 20),
    )(
        *[
            pltpu.with_memory_space_constraint(x, pltpu.HBM)
            for x in (pressure_start, along_start, cross_start, depth_layers, stiffness, lists, owner_map)
        ]
    )
    return (pressure, panels.reshape(1, slots, 1, STEPS // 2 * cols))


def solution(mesh):
    in_specs = (
        P("batch", None, "along", "cross"),
        P("batch", None, "along", "cross"),
        P("batch", None, "along", "cross"),
        P("along", "cross"),
        P("along", "cross"),
        P("batch", None),
        P(("along", "cross"), None),
    )
    out_specs = (P("batch", None, "along", "cross"), P(("along", "cross"), None, "batch", None))
    return jax.shard_map(shards, mesh=mesh, in_specs=in_specs, out_specs=out_specs, check_vma=False)
```

```python
import functools

import jax
import jax.numpy as jnp
from jax import lax
from jax.experimental import pallas as pl
from jax.experimental.pallas import tpu as pltpu
from jax.sharding import PartitionSpec as P

STEPS = 8
HALO = 8
PAD = 8
LAG = 3
MESH = pl.DeviceIdType.MESH


def kernel(
    n_along,
    layers,
    rows,
    cols,
    cap,
    p_hbm,
    fa_hbm,
    fc_hbm,
    d_hbm,
    k_hbm,
    lists_hbm,
    owners_hbm,
    out_p,
    landed,
    ep,
    ea,
    ec,
    dx,
    kx,
    lists,
    owners,
    place,
    trace,
    trace_out,
    outgoing,
    local_sem,
    halo_send,
    halo_recv,
    trace_send,
    trace_recv,
    panel_send,
    panel_recv,
    final_sem,
    round_sem,
):
    i = lax.axis_index("along")
    j = lax.axis_index("cross")
    other = 1 - j
    block = i * 2 + j
    n_owners = 2 * n_along
    half = rows // 2
    ext = half + HALO
    slots = n_owners * cap

    list_copy = pltpu.make_async_copy(lists_hbm, lists, local_sem.at[5])
    owner_copy = pltpu.make_async_copy(owners_hbm, owners, local_sem.at[6])
    list_copy.start()
    owner_copy.start()
    fields = ((p_hbm, ep), (fa_hbm, ea), (fc_hbm, ec), (d_hbm, dx), (k_hbm, kx))

    def take(src, start, count):
        if len(src.shape) == 4:
            return src.at[0, :, pl.ds(start, count), :]
        return src.at[pl.ds(start, count), :]

    def put(dst, side, start, count):
        if len(dst.shape) == 4:
            return dst.at[side, :, pl.ds(start, count), :]
        return dst.at[side, pl.ds(start, count), :]

    def first_row(core):
        return pl.multiple_of((half - HALO) * core, 8)

    def first_slot(core):
        return pl.multiple_of(PAD + HALO - HALO * core, 8)

    own_copies = []
    for index, (src, dst) in enumerate(fields):
        copy = pltpu.make_async_copy(
            take(src, first_row(j), ext), put(dst, j, first_slot(j), ext), local_sem.at[index]
        )
        copy.start()
        own_copies.append(copy)

    after_chip = lax.rem(i + 1, n_along)
    before_chip = lax.rem(i + n_along - 1, n_along)
    barrier = pltpu.get_barrier_semaphore()
    pl.semaphore_signal(barrier, inc=1, device_id={"cross": other}, device_id_type=MESH)
    for chip in (after_chip, before_chip):
        for core in range(2):
            pl.semaphore_signal(
                barrier, inc=1, device_id={"along": chip, "cross": core}, device_id_type=MESH
            )

    pl.semaphore_wait(barrier, 5)

    sends = []
    for index, (src, dst) in enumerate(fields):
        sends.append(
            pltpu.make_async_remote_copy(
                src_ref=take(src, rows - HALO, HALO),
                dst_ref=put(dst, j, PAD, HALO),
                send_sem=halo_send.at[index, 0],
                recv_sem=halo_recv.at[index, 1 + j],
                device_id={"along": after_chip, "cross": 0},
                device_id_type=MESH,
            )
        )
        sends.append(
            pltpu.make_async_remote_copy(
                src_ref=take(src, 0, HALO),
                dst_ref=put(dst, j, PAD + ext, HALO),
                send_sem=halo_send.at[index, 1],
                recv_sem=halo_recv.at[index, 1 + j],
                device_id={"along": before_chip, "cross": 1},
                device_id_type=MESH,
            )
        )
        sends.append(
            pltpu.make_async_remote_copy(
                src_ref=take(src, first_row(other), ext),
                dst_ref=put(dst, j, first_slot(other), ext),
                send_sem=halo_send.at[index, 2],
                recv_sem=halo_recv.at[index, 0],
                device_id={"cross": other},
                device_id_type=MESH,
            )
        )
    for copy in sends[0::3] + sends[1::3] + sends[2::3]:
        copy.start()

    rounds = max(1, n_along.bit_length() - 2)

    def tell(index):
        for away in (1 << index, n_along - (1 << index)):
            pl.semaphore_signal(
                round_sem.at[index],
                inc=1,
                device_id={"along": lax.rem(i + away, n_along)},
                device_id_type=MESH,
            )

    tell(0)

    for index, (src, dst) in enumerate(fields):
        if len(dst.shape) == 4:
            tail = PAD + ext + HALO
            dst[:, :, 0:PAD, :] = jnp.zeros((2, layers, PAD, cols), jnp.float32)
            dst[:, :, tail : tail + PAD, :] = jnp.zeros((2, layers, PAD, cols), jnp.float32)

    list_copy.wait()
    owner_copy.wait()
    patches = 2 * rows
    lane_r = lax.broadcasted_iota(jnp.int32, (patches, patches), 0)
    lane_c = lax.broadcasted_iota(jnp.int32, (patches, patches), 1)
    id_r = 2 * lax.rem(lane_r, rows) + lane_r // rows
    id_c = 2 * lax.rem(lane_c, rows) + lane_c // rows
    wanted = id_r + block * patches
    seen = jnp.zeros((patches, lists.shape[1]), jnp.float32)
    for row in range(lists.shape[0]):
        seen = jnp.where(lists[row : row + 1, :] == wanted, 1.0, seen)
    ones = jnp.ones((8, lists.shape[1]), jnp.bfloat16)
    member = lax.dot_general(
        ones, seen.astype(jnp.bfloat16), (((1,), (1,)), ((), ())), preferred_element_type=jnp.float32
    )
    permute = jnp.where(lane_r == id_c, 1.0, 0.0).astype(jnp.bfloat16)
    owner_rows = jnp.broadcast_to(owners[...].astype(jnp.float32), (8, patches)).astype(jnp.bfloat16)
    owner_of = jnp.dot(owner_rows, permute, preferred_element_type=jnp.float32)
    slot = lax.broadcasted_iota(jnp.int32, (slots, patches), 0)
    slot_owner = slot // cap
    slot_rank = (slot - slot_owner * cap).astype(jnp.float32)
    mine = owner_of[0:1, :] == slot_owner.astype(jnp.float32)
    before = jnp.where(id_r < id_c, 1.0, 0.0).astype(jnp.bfloat16)
    rank = jnp.dot(
        jnp.where(mine, 1.0, 0.0).astype(jnp.bfloat16), before, preferred_element_type=jnp.float32
    )
    held = jnp.where(mine & (rank == slot_rank), jnp.where(member[0:1, :] > 0.5, 1.0, 0.0), 0.0)
    place[...] = held.astype(jnp.bfloat16)

    lane = lax.broadcasted_iota(jnp.int32, (8, cols), 1)
    first_lane = lane == 0
    last_lane = lane == cols - 1
    low_lanes = lax.broadcasted_iota(jnp.int32, (rows, cols), 1) < cols // 2
    zero = jnp.zeros((8, cols), jnp.float32)
    tiles = (half + 2 * HALO) // 8
    own_tiles = range(HALO // 8, HALO // 8 + half // 8)
    own_start = pl.multiple_of(half * j, 8)

    def trace_copy(t):
        return pltpu.make_async_remote_copy(
            src_ref=trace_out.at[t],
            dst_ref=trace.at[t, pl.ds(own_start, half), :],
            send_sem=trace_send.at[t],
            recv_sem=trace_recv.at[t],
            device_id={"cross": other},
            device_id_type=MESH,
        )

    def piece(t, flow_tiles, pressure_tiles):
        def rows_of(tile):
            r = PAD + 8 * tile
            return r, slice(r, r + 8)

        def flows(tile):
            r, at = rows_of(tile)
            depth = [dx[h, at, :] for h in range(2)]
            ready = {}
            for tick in range(layers + LAG):
                if tick < layers:
                    pressure = [ep[h, tick, at, :] for h in range(2)]
                    ready[tick] = (
                        pressure,
                        [pltpu.roll(pressure[h], cols - 1, 1) for h in range(2)],
                    )
                z = tick - LAG
                if z >= 0:
                    pressure, turned = ready.pop(z)
                    right = [
                        jnp.where(last_lane, turned[1], turned[0]),
                        jnp.where(last_lane, 0.0, turned[1]),
                    ]
                    for h in range(2):
                        wet = depth[h] > z
                        ahead = ep[h, z, r + 1 : r + 9, :]
                        ea[h, z, at, :] = jnp.where(
                            wet, ea[h, z, at, :] - (ahead - pressure[h]), 0.0
                        )
                        ec[h, z, at, :] = jnp.where(
                            wet, ec[h, z, at, :] - (right[h] - pressure[h]), 0.0
                        )
                yield

        def pressures(tile):
            r, at = rows_of(tile)
            depth = [dx[h, at, :] for h in range(2)]
            stiff = [kx[h, at, :] for h in range(2)]
            half_stiff = [0.5 * stiff[h] for h in range(2)]
            pressure = [ep[h, 0, at, :] for h in range(2)]
            wet = [depth[h] > 0 for h in range(2)]
            down = [zero, zero]
            seafloor = [zero, zero]
            ready = {}
            for tick in range(layers + LAG):
                if tick < layers:
                    cross = [ec[h, tick, at, :] for h in range(2)]
                    ready[tick] = (cross, [pltpu.roll(cross[h], 1, 1) for h in range(2)])
                z = tick - LAG
                if z >= 0:
                    cross, turned = ready.pop(z)
                    left = [
                        jnp.where(first_lane, 0.0, turned[0]),
                        jnp.where(first_lane, turned[0], turned[1]),
                    ]
                    for h in range(2):
                        spread = (ea[h, z, at, :] - ea[h, z, r - 1 : r + 7, :]) + (
                            cross[h] - left[h]
                        )
                        if z + 1 < layers:
                            lower = ep[h, z + 1, at, :]
                            wet_lower = depth[h] > z + 1
                            up = jnp.where(wet_lower, lower - pressure[h], 0.0)
                            vertical = up - down[h]
                        else:
                            vertical = -down[h]
                        value = pressure[h] - stiff[h] * spread + half_stiff[h] * vertical
                        value = jnp.where(wet[h], value, 0.0)
                        ep[h, z, at, :] = value
                        if tile in own_tiles:
                            seafloor[h] = jnp.where(wet[h], value, seafloor[h])
                        if z + 1 < layers:
                            pressure[h], wet[h], down[h] = lower, wet_lower, up
                yield
            if tile in own_tiles:
                to = 8 * (tile - HALO // 8)
                trace[t, pl.ds(pl.multiple_of(own_start + to, 8), 8), :] = jnp.where(
                    j == 0, seafloor[0], seafloor[1]
                )
                trace_out[t, to : to + 8, :] = jnp.where(j == 0, seafloor[1], seafloor[0])

        for tile in range(tiles + 1):
            work = []
            if tile in flow_tiles:
                work.append(flows(tile))
            if tile - 1 in pressure_tiles:
                work.append(pressures(tile - 1))
            for _ in range(layers + LAG + 1):
                for part in work:
                    next(part, None)
            if tile - 1 == own_tiles[-1] and len(pressure_tiles) == tiles:
                trace_copy(t).start()

    def step(t):
        piece(t, range(tiles), range(tiles))

    def early(t):
        @pl.when(j == 0)
        def _():
            piece(t, range(t + 1, tiles), range(t + 2, tiles))

        @pl.when(j == 1)
        def _():
            piece(t, range(tiles - 2 - t), range(tiles - 2 - t))

    def late(t):
        @pl.when(j == 0)
        def _():
            piece(t, range(t + 1), range(t + 2))

        @pl.when(j == 1)
        def _():
            piece(t, range(tiles - 2 - t, tiles), range(tiles - 2 - t, tiles))

        trace_copy(t).start()

    def arrived(sources):
        for index, (src, dst) in enumerate(fields):
            for source in sources:
                count = ext if source == 0 else HALO
                pltpu.make_async_copy(
                    take(src, 0, count), put(dst, 0, PAD, count), halo_recv.at[index, source]
                ).wait()

    pl.semaphore_wait(round_sem.at[0], 2)
    tell(1)
    for copy in own_copies:
        copy.wait()
    arrived((0,))
    early(0)
    pl.semaphore_wait(round_sem.at[1], 2)
    tell(2)
    early(1)
    for index in range(3, rounds):
        pl.semaphore_wait(round_sem.at[index - 1], 2)
        tell(index)
    arrived((1, 2))

    @pl.when((i == 0) & (j == 0))
    def _():
        ep[:, :, PAD : PAD + HALO, :] = jnp.zeros((2, layers, HALO, cols), jnp.float32)
        dx[:, PAD : PAD + HALO, :] = jnp.zeros((2, HALO, cols), jnp.int32)

    @pl.when((i == n_along - 1) & (j == 1))
    def _():
        ep[:, :, PAD + ext : PAD + ext + HALO, :] = jnp.zeros((2, layers, HALO, cols), jnp.float32)
        dx[:, PAD + ext : PAD + ext + HALO, :] = jnp.zeros((2, HALO, cols), jnp.int32)

    order = []
    for away in range(n_along // 2, 0, -1):
        order += [away] if away == n_along // 2 else [away, n_along - away]
    targets = [(lax.rem(i + away, n_along), core) for away in order for core in (j, other)]
    targets.append((i, other))

    def panel_copy(g, target):
        chip, core = target
        return pltpu.make_async_remote_copy(
            src_ref=outgoing.at[g, pl.ds((2 * chip + core) * cap, cap)],
            dst_ref=landed.at[g, pl.ds(block * cap, cap)],
            send_sem=panel_send.at[g],
            recv_sem=panel_recv.at[g],
            device_id={"along": chip, "cross": core},
            device_id_type=MESH,
        )

    def own_panel_copy(g):
        return pltpu.make_async_copy(
            outgoing.at[g, pl.ds(block * cap, cap)],
            landed.at[g, pl.ds(block * cap, cap)],
            final_sem.at[2 + g],
        )

    def fill_group(g):
        for s in range(2):
            trace_copy(2 * g + s).wait_recv()
        first, second = trace[2 * g], trace[2 * g + 1]
        left = jnp.where(low_lanes, first, pltpu.roll(second, cols // 2, 1))
        right = jnp.where(low_lanes, pltpu.roll(first, cols // 2, 1), second)
        rest = jnp.concatenate([left, right], 0)
        total = None
        for part in range(3):
            piece = rest.astype(jnp.bfloat16)
            term = jnp.dot(place[...], piece, preferred_element_type=jnp.float32)
            total = term if total is None else total + term
            rest = rest - piece.astype(jnp.float32)
        outgoing[g, :, 0, :] = total
        own_panel_copy(g).start()

    def group_sends(g):
        return [functools.partial(lambda target: panel_copy(g, target).start(), t) for t in targets]

    own_pressure = pltpu.make_async_copy(
        ep.at[j, :, pl.ds(PAD + HALO, half), :],
        out_p.at[0, :, pl.ds(own_start, half), :],
        final_sem.at[0],
    )
    other_pressure = pltpu.make_async_remote_copy(
        src_ref=ep.at[other, :, pl.ds(PAD + HALO, half), :],
        dst_ref=out_p.at[0, :, pl.ds(own_start, half), :],
        send_sem=final_sem.at[1],
        recv_sem=final_sem.at[6],
        device_id={"cross": other},
        device_id_type=MESH,
    )

    def advance(g, carry):
        step(2 * g + 2)
        fill_group(g)
        for emit in group_sends(g):
            emit()
        step(2 * g + 3)
        return carry

    groups = STEPS // 2
    late(0)
    late(1)
    pl.semaphore_wait(round_sem.at[rounds - 1], 2)
    lax.fori_loop(0, groups - 1, advance, 0)
    fill_group(groups - 1)
    for emit in group_sends(groups - 1):
        emit()
    other_pressure.start()
    own_pressure.start()

    for copy in sends:
        copy.wait_send()
    for t in range(STEPS):
        trace_copy(t).wait_send()
    own_pressure.wait()
    other_pressure.wait()
    moved = (n_owners - 1) * cap
    for g in range(groups):
        own_panel_copy(g).wait()
        for sem in (panel_recv, panel_send):
            pltpu.make_async_copy(
                outgoing.at[g, pl.ds(0, moved)], landed.at[g, pl.ds(0, moved)], sem.at[g]
            ).wait()


def store(pressure, panels, out_p, out_s, sem):
    copies = [pltpu.make_async_copy(pressure, out_p, sem.at[panels.shape[0]])]
    for g in range(panels.shape[0]):
        copies.append(pltpu.make_async_copy(panels.at[g], out_s.at[:, g], sem.at[g]))
    for copy in copies:
        copy.start()
    for copy in copies:
        copy.wait()


def shards(
    pressure_start, along_start, cross_start, depth_layers, stiffness, patch_lists, owner_map
):
    _, layers, rows, cols = pressure_start.shape
    n_along = lax.axis_size("along")
    n_owners = n_along * lax.axis_size("cross")
    cap = 2 * rows // n_owners + 1
    slots = n_owners * cap
    ext_rows = rows // 2 + 2 * HALO + 2 * PAD
    lists = patch_lists.reshape(-1, cols)
    any_space = pl.BlockSpec(memory_space=pl.ANY)
    pressure, panels = pl.pallas_call(
        functools.partial(kernel, n_along, layers, rows, cols, cap),
        out_shape=(
            jax.ShapeDtypeStruct(pressure_start.shape, jnp.float32),
            jax.ShapeDtypeStruct((STEPS // 2, slots, 1, cols), jnp.float32),
        ),
        in_specs=[any_space] * 7,
        out_specs=(any_space, any_space),
        scratch_shapes=[
            pltpu.VMEM((2, layers, ext_rows, cols), jnp.float32),
            pltpu.VMEM((2, layers, ext_rows, cols), jnp.float32),
            pltpu.VMEM((2, layers, ext_rows, cols), jnp.float32),
            pltpu.VMEM((2, ext_rows, cols), jnp.int32),
            pltpu.VMEM((2, ext_rows, cols), jnp.float32),
            pltpu.VMEM(lists.shape, jnp.int32),
            pltpu.VMEM(owner_map.shape, jnp.int32),
            pltpu.VMEM((slots, 2 * rows), jnp.bfloat16),
            pltpu.VMEM((STEPS, rows, cols), jnp.float32),
            pltpu.VMEM((STEPS, rows // 2, cols), jnp.float32),
            pltpu.VMEM((STEPS // 2, slots, 1, cols), jnp.float32),
            pltpu.SemaphoreType.DMA((7,)),
            pltpu.SemaphoreType.DMA((5, 3)),
            pltpu.SemaphoreType.DMA((5, 3)),
            pltpu.SemaphoreType.DMA((STEPS,)),
            pltpu.SemaphoreType.DMA((STEPS,)),
            pltpu.SemaphoreType.DMA((STEPS // 2,)),
            pltpu.SemaphoreType.DMA((STEPS // 2,)),
            pltpu.SemaphoreType.DMA((7,)),
            pltpu.SemaphoreType.REGULAR((max(1, n_along.bit_length() - 2),)),
        ],
        compiler_params=pltpu.CompilerParams(collective_id=0, has_side_effects=True, vmem_limit_bytes=16 << 20),
    )(
        *[
            pltpu.with_memory_space_constraint(x, pltpu.HBM)
            for x in (pressure_start, along_start, cross_start, depth_layers, stiffness, lists, owner_map)
        ]
    )
    pressure, panels = pl.pallas_call(
        store,
        out_shape=(
            jax.ShapeDtypeStruct(pressure.shape, jnp.float32),
            jax.ShapeDtypeStruct((slots, STEPS // 2, 1, cols), jnp.float32),
        ),
        in_specs=[any_space] * 2,
        out_specs=(any_space, any_space),
        scratch_shapes=[pltpu.SemaphoreType.DMA((STEPS // 2 + 1,))],
        compiler_params=pltpu.CompilerParams(vmem_limit_bytes=1 << 20),
    )(pressure, panels)
    return (pressure, panels.reshape(1, slots, 1, STEPS // 2 * cols))


def solution(mesh):
    in_specs = (
        P("batch", None, "along", "cross"),
        P("batch", None, "along", "cross"),
        P("batch", None, "along", "cross"),
        P("along", "cross"),
        P("along", "cross"),
        P("batch", None),
        P(("along", "cross"), None),
    )
    out_specs = (P("batch", None, "along", "cross"), P(("along", "cross"), None, "batch", None))
    return jax.shard_map(shards, mesh=mesh, in_specs=in_specs, out_specs=out_specs, check_vma=False)
```

```python
import functools

import jax
import jax.numpy as jnp
from jax import lax
from jax.experimental import pallas as pl
from jax.experimental.pallas import tpu as pltpu
from jax.sharding import PartitionSpec as P

STEPS = 8
HALO = 8
PAD = 8
LAG = 3
MESH = pl.DeviceIdType.MESH


def kernel(
    n_along,
    layers,
    rows,
    cols,
    cap,
    p_hbm,
    fa_hbm,
    fc_hbm,
    d_hbm,
    k_hbm,
    lists_hbm,
    owners_hbm,
    out_p,
    landed,
    ep,
    ea,
    ec,
    dx,
    kx,
    lists,
    owners,
    place,
    trace,
    trace_out,
    outgoing,
    local_sem,
    halo_send,
    halo_recv,
    trace_send,
    trace_recv,
    panel_send,
    panel_recv,
    final_sem,
    round_sem,
):
    i = lax.axis_index("along")
    j = lax.axis_index("cross")
    other = 1 - j
    block = i * 2 + j
    n_owners = 2 * n_along
    half = rows // 2
    ext = half + HALO
    slots = n_owners * cap

    list_copy = pltpu.make_async_copy(lists_hbm, lists, local_sem.at[5])
    owner_copy = pltpu.make_async_copy(owners_hbm, owners, local_sem.at[6])
    list_copy.start()
    owner_copy.start()
    fields = ((p_hbm, ep), (fa_hbm, ea), (fc_hbm, ec), (d_hbm, dx), (k_hbm, kx))

    def take(src, start, count):
        if len(src.shape) == 4:
            return src.at[0, :, pl.ds(start, count), :]
        return src.at[pl.ds(start, count), :]

    def put(dst, side, start, count):
        if len(dst.shape) == 4:
            return dst.at[side, :, pl.ds(start, count), :]
        return dst.at[side, pl.ds(start, count), :]

    def first_row(core):
        return pl.multiple_of((half - HALO) * core, 8)

    def first_slot(core):
        return pl.multiple_of(PAD + HALO - HALO * core, 8)

    own_copies = []
    for index, (src, dst) in enumerate(fields):
        copy = pltpu.make_async_copy(
            take(src, first_row(j), ext), put(dst, j, first_slot(j), ext), local_sem.at[index]
        )
        copy.start()
        own_copies.append(copy)

    after_chip = lax.rem(i + 1, n_along)
    before_chip = lax.rem(i + n_along - 1, n_along)
    barrier = pltpu.get_barrier_semaphore()
    pl.semaphore_signal(barrier, inc=1, device_id={"cross": other}, device_id_type=MESH)
    for chip in (after_chip, before_chip):
        for core in range(2):
            pl.semaphore_signal(
                barrier, inc=1, device_id={"along": chip, "cross": core}, device_id_type=MESH
            )

    pl.semaphore_wait(barrier, 5)

    sends = []
    for index, (src, dst) in enumerate(fields):
        sends.append(
            pltpu.make_async_remote_copy(
                src_ref=take(src, rows - HALO, HALO),
                dst_ref=put(dst, j, PAD, HALO),
                send_sem=halo_send.at[index, 0],
                recv_sem=halo_recv.at[index, 1 + j],
                device_id={"along": after_chip, "cross": 0},
                device_id_type=MESH,
            )
        )
        sends.append(
            pltpu.make_async_remote_copy(
                src_ref=take(src, 0, HALO),
                dst_ref=put(dst, j, PAD + ext, HALO),
                send_sem=halo_send.at[index, 1],
                recv_sem=halo_recv.at[index, 1 + j],
                device_id={"along": before_chip, "cross": 1},
                device_id_type=MESH,
            )
        )
        sends.append(
            pltpu.make_async_remote_copy(
                src_ref=take(src, first_row(other), ext),
                dst_ref=put(dst, j, first_slot(other), ext),
                send_sem=halo_send.at[index, 2],
                recv_sem=halo_recv.at[index, 0],
                device_id={"cross": other},
                device_id_type=MESH,
            )
        )
    for copy in sends[0::3] + sends[1::3] + sends[2::3]:
        copy.start()

    rounds = max(1, n_along.bit_length() - 2)

    def tell(index):
        for away in (1 << index, n_along - (1 << index)):
            pl.semaphore_signal(
                round_sem.at[index],
                inc=1,
                device_id={"along": lax.rem(i + away, n_along)},
                device_id_type=MESH,
            )

    tell(0)

    for index, (src, dst) in enumerate(fields):
        if len(dst.shape) == 4:
            tail = PAD + ext + HALO
            dst[:, :, 0:PAD, :] = jnp.zeros((2, layers, PAD, cols), jnp.float32)
            dst[:, :, tail : tail + PAD, :] = jnp.zeros((2, layers, PAD, cols), jnp.float32)

    list_copy.wait()
    owner_copy.wait()
    patches = 2 * rows
    lane_r = lax.broadcasted_iota(jnp.int32, (patches, patches), 0)
    lane_c = lax.broadcasted_iota(jnp.int32, (patches, patches), 1)
    id_r = 2 * lax.rem(lane_r, rows) + lane_r // rows
    id_c = 2 * lax.rem(lane_c, rows) + lane_c // rows
    wanted = id_r + block * patches
    seen = jnp.zeros((patches, lists.shape[1]), jnp.float32)
    for row in range(lists.shape[0]):
        seen = jnp.where(lists[row : row + 1, :] == wanted, 1.0, seen)
    ones = jnp.ones((8, lists.shape[1]), jnp.bfloat16)
    member = lax.dot_general(
        ones, seen.astype(jnp.bfloat16), (((1,), (1,)), ((), ())), preferred_element_type=jnp.float32
    )
    permute = jnp.where(lane_r == id_c, 1.0, 0.0).astype(jnp.bfloat16)
    owner_rows = jnp.broadcast_to(owners[...].astype(jnp.float32), (8, patches)).astype(jnp.bfloat16)
    owner_of = jnp.dot(owner_rows, permute, preferred_element_type=jnp.float32)
    slot = lax.broadcasted_iota(jnp.int32, (slots, patches), 0)
    slot_owner = slot // cap
    slot_rank = (slot - slot_owner * cap).astype(jnp.float32)
    mine = owner_of[0:1, :] == slot_owner.astype(jnp.float32)
    before = jnp.where(id_r < id_c, 1.0, 0.0).astype(jnp.bfloat16)
    rank = jnp.dot(
        jnp.where(mine, 1.0, 0.0).astype(jnp.bfloat16), before, preferred_element_type=jnp.float32
    )
    held = jnp.where(mine & (rank == slot_rank), jnp.where(member[0:1, :] > 0.5, 1.0, 0.0), 0.0)
    place[...] = held.astype(jnp.bfloat16)

    lane = lax.broadcasted_iota(jnp.int32, (8, cols), 1)
    first_lane = lane == 0
    last_lane = lane == cols - 1
    low_lanes = lax.broadcasted_iota(jnp.int32, (rows, cols), 1) < cols // 2
    zero = jnp.zeros((8, cols), jnp.float32)
    tiles = (half + 2 * HALO) // 8
    own_tiles = range(HALO // 8, HALO // 8 + half // 8)
    own_start = pl.multiple_of(half * j, 8)

    def trace_copy(t):
        return pltpu.make_async_remote_copy(
            src_ref=trace_out.at[t],
            dst_ref=trace.at[t, pl.ds(own_start, half), :],
            send_sem=trace_send.at[t],
            recv_sem=trace_recv.at[t],
            device_id={"cross": other},
            device_id_type=MESH,
        )

    def piece(t, flow_tiles, pressure_tiles):
        def rows_of(tile):
            r = PAD + 8 * tile
            return r, slice(r, r + 8)

        def flows(tile):
            r, at = rows_of(tile)
            depth = [dx[h, at, :] for h in range(2)]
            ready = {}
            for tick in range(layers + LAG):
                if tick < layers:
                    pressure = [ep[h, tick, at, :] for h in range(2)]
                    ready[tick] = (
                        pressure,
                        [pltpu.roll(pressure[h], cols - 1, 1) for h in range(2)],
                    )
                z = tick - LAG
                if z >= 0:
                    pressure, turned = ready.pop(z)
                    right = [
                        jnp.where(last_lane, turned[1], turned[0]),
                        jnp.where(last_lane, 0.0, turned[1]),
                    ]
                    for h in range(2):
                        wet = depth[h] > z
                        ahead = ep[h, z, r + 1 : r + 9, :]
                        ea[h, z, at, :] = jnp.where(
                            wet, ea[h, z, at, :] - (ahead - pressure[h]), 0.0
                        )
                        ec[h, z, at, :] = jnp.where(
                            wet, ec[h, z, at, :] - (right[h] - pressure[h]), 0.0
                        )
                yield

        def pressures(tile):
            r, at = rows_of(tile)
            depth = [dx[h, at, :] for h in range(2)]
            stiff = [kx[h, at, :] for h in range(2)]
            half_stiff = [0.5 * stiff[h] for h in range(2)]
            pressure = [ep[h, 0, at, :] for h in range(2)]
            wet = [depth[h] > 0 for h in range(2)]
            down = [zero, zero]
            seafloor = [zero, zero]
            ready = {}
            for tick in range(layers + LAG):
                if tick < layers:
                    cross = [ec[h, tick, at, :] for h in range(2)]
                    ready[tick] = (cross, [pltpu.roll(cross[h], 1, 1) for h in range(2)])
                z = tick - LAG
                if z >= 0:
                    cross, turned = ready.pop(z)
                    left = [
                        jnp.where(first_lane, 0.0, turned[0]),
                        jnp.where(first_lane, turned[0], turned[1]),
                    ]
                    for h in range(2):
                        spread = (ea[h, z, at, :] - ea[h, z, r - 1 : r + 7, :]) + (
                            cross[h] - left[h]
                        )
                        if z + 1 < layers:
                            lower = ep[h, z + 1, at, :]
                            wet_lower = depth[h] > z + 1
                            up = jnp.where(wet_lower, lower - pressure[h], 0.0)
                            vertical = up - down[h]
                        else:
                            vertical = -down[h]
                        value = pressure[h] - stiff[h] * spread + half_stiff[h] * vertical
                        value = jnp.where(wet[h], value, 0.0)
                        ep[h, z, at, :] = value
                        if tile in own_tiles:
                            seafloor[h] = jnp.where(wet[h], value, seafloor[h])
                        if z + 1 < layers:
                            pressure[h], wet[h], down[h] = lower, wet_lower, up
                yield
            if tile in own_tiles:
                to = 8 * (tile - HALO // 8)
                trace[t, pl.ds(pl.multiple_of(own_start + to, 8), 8), :] = jnp.where(
                    j == 0, seafloor[0], seafloor[1]
                )
                trace_out[t, to : to + 8, :] = jnp.where(j == 0, seafloor[1], seafloor[0])

        for tile in range(tiles + 1):
            work = []
            if tile in flow_tiles:
                work.append(flows(tile))
            if tile - 1 in pressure_tiles:
                work.append(pressures(tile - 1))
            for _ in range(layers + LAG + 1):
                for part in work:
                    next(part, None)
            if tile - 1 == own_tiles[-1] and len(pressure_tiles) == tiles:
                trace_copy(t).start()

    def step(t):
        piece(t, range(tiles), range(tiles))

    def early(t):
        @pl.when(j == 0)
        def _():
            piece(t, range(t + 1, tiles), range(t + 2, tiles))

        @pl.when(j == 1)
        def _():
            piece(t, range(tiles - 2 - t), range(tiles - 2 - t))

    def late(t):
        @pl.when(j == 0)
        def _():
            piece(t, range(t + 1), range(t + 2))

        @pl.when(j == 1)
        def _():
            piece(t, range(tiles - 2 - t, tiles), range(tiles - 2 - t, tiles))

        trace_copy(t).start()

    def arrived(sources):
        for index, (src, dst) in enumerate(fields):
            for source in sources:
                count = ext if source == 0 else HALO
                pltpu.make_async_copy(
                    take(src, 0, count), put(dst, 0, PAD, count), halo_recv.at[index, source]
                ).wait()

    pl.semaphore_wait(round_sem.at[0], 2)
    tell(1)
    for copy in own_copies:
        copy.wait()
    arrived((0,))
    early(0)
    pl.semaphore_wait(round_sem.at[1], 2)
    tell(2)
    early(1)
    for index in range(3, rounds):
        pl.semaphore_wait(round_sem.at[index - 1], 2)
        tell(index)
    arrived((1, 2))

    @pl.when((i == 0) & (j == 0))
    def _():
        ep[:, :, PAD : PAD + HALO, :] = jnp.zeros((2, layers, HALO, cols), jnp.float32)
        dx[:, PAD : PAD + HALO, :] = jnp.zeros((2, HALO, cols), jnp.int32)

    @pl.when((i == n_along - 1) & (j == 1))
    def _():
        ep[:, :, PAD + ext : PAD + ext + HALO, :] = jnp.zeros((2, layers, HALO, cols), jnp.float32)
        dx[:, PAD + ext : PAD + ext + HALO, :] = jnp.zeros((2, HALO, cols), jnp.int32)

    order = []
    for away in range(n_along // 2, 0, -1):
        order += [away] if away == n_along // 2 else [away, n_along - away]
    targets = [(lax.rem(i + away, n_along), core) for away in order for core in (j, other)]
    targets.append((i, other))

    def panel_copy(g, target):
        chip, core = target
        return pltpu.make_async_remote_copy(
            src_ref=outgoing.at[g, pl.ds((2 * chip + core) * cap, cap)],
            dst_ref=landed.at[g, pl.ds(block * cap, cap)],
            send_sem=panel_send.at[g],
            recv_sem=panel_recv.at[g],
            device_id={"along": chip, "cross": core},
            device_id_type=MESH,
        )

    def own_panel_copy(g):
        return pltpu.make_async_copy(
            outgoing.at[g, pl.ds(block * cap, cap)],
            landed.at[g, pl.ds(block * cap, cap)],
            final_sem.at[2 + g],
        )

    def fill_group(g):
        for s in range(2):
            trace_copy(2 * g + s).wait_recv()
        first, second = trace[2 * g], trace[2 * g + 1]
        left = jnp.where(low_lanes, first, pltpu.roll(second, cols // 2, 1))
        right = jnp.where(low_lanes, pltpu.roll(first, cols // 2, 1), second)
        rest = jnp.concatenate([left, right], 0)
        total = None
        for part in range(3):
            piece = rest.astype(jnp.bfloat16)
            term = jnp.dot(place[...], piece, preferred_element_type=jnp.float32)
            total = term if total is None else total + term
            rest = rest - piece.astype(jnp.float32)
        outgoing[g, :, 0, :] = total
        own_panel_copy(g).start()

    def group_sends(g):
        return [functools.partial(lambda target: panel_copy(g, target).start(), t) for t in targets]

    own_pressure = pltpu.make_async_copy(
        ep.at[j, :, pl.ds(PAD + HALO, half), :],
        out_p.at[0, :, pl.ds(own_start, half), :],
        final_sem.at[0],
    )
    other_pressure = pltpu.make_async_remote_copy(
        src_ref=ep.at[other, :, pl.ds(PAD + HALO, half), :],
        dst_ref=out_p.at[0, :, pl.ds(own_start, half), :],
        send_sem=final_sem.at[1],
        recv_sem=final_sem.at[6],
        device_id={"cross": other},
        device_id_type=MESH,
    )

    def advance(g, carry):
        step(2 * g + 2)
        fill_group(g)
        for emit in group_sends(g):
            emit()
        step(2 * g + 3)
        return carry

    groups = STEPS // 2
    late(0)
    late(1)
    pl.semaphore_wait(round_sem.at[rounds - 1], 2)
    lax.fori_loop(0, groups - 2, advance, 0)
    step(STEPS - 2)
    fill_group(groups - 2)
    for emit in group_sends(groups - 2):
        emit()
    piece(STEPS - 1, range(tiles - 1), own_tiles)
    trace_copy(STEPS - 1).start()
    fill_group(groups - 1)
    for emit in group_sends(groups - 1):
        emit()
    other_pressure.start()
    own_pressure.start()

    for copy in sends:
        copy.wait_send()
    for t in range(STEPS):
        trace_copy(t).wait_send()
    own_pressure.wait()
    other_pressure.wait()
    moved = (n_owners - 1) * cap
    for g in range(groups):
        own_panel_copy(g).wait()
        for sem in (panel_recv, panel_send):
            pltpu.make_async_copy(
                outgoing.at[g, pl.ds(0, moved)], landed.at[g, pl.ds(0, moved)], sem.at[g]
            ).wait()


def store(pressure, panels, out_p, out_s, sem):
    copies = [pltpu.make_async_copy(pressure, out_p, sem.at[panels.shape[0]])]
    for g in range(panels.shape[0]):
        copies.append(pltpu.make_async_copy(panels.at[g], out_s.at[:, g], sem.at[g]))
    for copy in copies:
        copy.start()
    for copy in copies:
        copy.wait()


def shards(
    pressure_start, along_start, cross_start, depth_layers, stiffness, patch_lists, owner_map
):
    _, layers, rows, cols = pressure_start.shape
    n_along = lax.axis_size("along")
    n_owners = n_along * lax.axis_size("cross")
    cap = 2 * rows // n_owners + 1
    slots = n_owners * cap
    ext_rows = rows // 2 + 2 * HALO + 2 * PAD
    lists = patch_lists.reshape(-1, cols)
    any_space = pl.BlockSpec(memory_space=pl.ANY)
    pressure, panels = pl.pallas_call(
        functools.partial(kernel, n_along, layers, rows, cols, cap),
        out_shape=(
            jax.ShapeDtypeStruct(pressure_start.shape, jnp.float32),
            jax.ShapeDtypeStruct((STEPS // 2, slots, 1, cols), jnp.float32),
        ),
        in_specs=[any_space] * 7,
        out_specs=(any_space, any_space),
        scratch_shapes=[
            pltpu.VMEM((2, layers, ext_rows, cols), jnp.float32),
            pltpu.VMEM((2, layers, ext_rows, cols), jnp.float32),
            pltpu.VMEM((2, layers, ext_rows, cols), jnp.float32),
            pltpu.VMEM((2, ext_rows, cols), jnp.int32),
            pltpu.VMEM((2, ext_rows, cols), jnp.float32),
            pltpu.VMEM(lists.shape, jnp.int32),
            pltpu.VMEM(owner_map.shape, jnp.int32),
            pltpu.VMEM((slots, 2 * rows), jnp.bfloat16),
            pltpu.VMEM((STEPS, rows, cols), jnp.float32),
            pltpu.VMEM((STEPS, rows // 2, cols), jnp.float32),
            pltpu.VMEM((STEPS // 2, slots, 1, cols), jnp.float32),
            pltpu.SemaphoreType.DMA((7,)),
            pltpu.SemaphoreType.DMA((5, 3)),
            pltpu.SemaphoreType.DMA((5, 3)),
            pltpu.SemaphoreType.DMA((STEPS,)),
            pltpu.SemaphoreType.DMA((STEPS,)),
            pltpu.SemaphoreType.DMA((STEPS // 2,)),
            pltpu.SemaphoreType.DMA((STEPS // 2,)),
            pltpu.SemaphoreType.DMA((7,)),
            pltpu.SemaphoreType.REGULAR((max(1, n_along.bit_length() - 2),)),
        ],
        compiler_params=pltpu.CompilerParams(collective_id=0, has_side_effects=True, vmem_limit_bytes=16 << 20),
    )(
        *[
            pltpu.with_memory_space_constraint(x, pltpu.HBM)
            for x in (pressure_start, along_start, cross_start, depth_layers, stiffness, lists, owner_map)
        ]
    )
    pressure, panels = pl.pallas_call(
        store,
        out_shape=(
            jax.ShapeDtypeStruct(pressure.shape, jnp.float32),
            jax.ShapeDtypeStruct((slots, STEPS // 2, 1, cols), jnp.float32),
        ),
        in_specs=[any_space] * 2,
        out_specs=(any_space, any_space),
        scratch_shapes=[pltpu.SemaphoreType.DMA((STEPS // 2 + 1,))],
        compiler_params=pltpu.CompilerParams(vmem_limit_bytes=1 << 20),
    )(pressure, panels)
    return (pressure, panels.reshape(1, slots, 1, STEPS // 2 * cols))


def solution(mesh):
    in_specs = (
        P("batch", None, "along", "cross"),
        P("batch", None, "along", "cross"),
        P("batch", None, "along", "cross"),
        P("along", "cross"),
        P("along", "cross"),
        P("batch", None),
        P(("along", "cross"), None),
    )
    out_specs = (P("batch", None, "along", "cross"), P(("along", "cross"), None, "batch", None))
    return jax.shard_map(shards, mesh=mesh, in_specs=in_specs, out_specs=out_specs, check_vma=False)
```
